256 devices in a mesh: gx: 32 (over z, x_hi, core), gy: 8 (over x_lo, y).
Axes of the slice: x: 4 (x_hi: 2, x_lo: 2; x = x_hi * 2 + x_lo), y: 4, z: 8, core: 2. Of those that a mesh axis runs over, the one named last changes fastest.
Arguments:
- conc: float32 [32, 2048, 1024], P(None, 'gx', 'gy'), may hold values from -4 to 4
- mobility: float32 [32, 2048, 1024], P(None, 'gx', 'gy'), may hold values from 0.3 to 3
- block_x: float32 [32, 2048, 64], P(None, 'gx'), may hold values from -0.75 to 0.75
- spike_x: float32 [32, 2048, 4], P(None, 'gx'), may hold values from -3 to 3
- reduced_x: float32 [32, 128, 128], replicated, may hold values from -0.5 to 0.5
- block_y: float32 [32, 1024, 128], P(None, 'gy'), may hold values from -0.5 to 0.5
- spike_y: float32 [32, 1024, 4], P(None, 'gy'), may hold values from -3 to 3
- reduced_y: float32 [32, 32, 32], replicated, may hold values from -1 to 1
Outputs:
- conc_next: float32 [32, 2048, 1024], P(None, 'gx', 'gy')
The draws below stay inside these ranges and needn't reach their ends.
All inputs are finite; a program needn't handle non-finite values.
Results may differ from the reference program's by a relative error of at most 0.00012.
Values sent between devices are 32-bit elements; how exact they have to be, the bound alone decides.
No kernel may reach another device: no remote copies, remote signals or barrier semaphores. Data moves between devices by JAX's collectives and lax.ppermute only.
A program may use at most 64 MiB of HBM per device.

```python
import math
import jax
import jax.numpy as jnp
from jax import lax

NZ = 32
CX = 64
CY = 128
NX = 2048
NY = 1024
RX = 128
RY = 32


def steps_of(key, shape, split, least, high):
    level, own = 1.0, jax.random.fold_in(key, 6)
    for axis_at, parts in split:
        heights = jnp.exp(jax.random.uniform(jax.random.fold_in(own, axis_at), (parts,), jnp.float32, least / len(split), high / len(split)))
        level = level * jnp.repeat(heights, shape[axis_at] // parts).reshape([-1 if axis == axis_at else 1 for axis in range(len(shape))])
    return level


def normal_values(stream_key, dims, deviation, bound, cuts=(), held_as=jnp.bfloat16):
    level = steps_of(stream_key, dims, cuts, -0.22, 0.18) if cuts else 1.0
    result = jax.random.normal(stream_key, dims, jnp.float32) * deviation * level
    return jnp.minimum(jnp.maximum(result, -bound), bound).astype(held_as)


def setup_inputs(seed: int = 0) -> dict:
    seeds = jax.random.split(jax.random.key(seed), 9)
    conc = normal_values(seeds[0], (NZ, NX, NY), 0.7, 4.0, ((1, 32), (2, 8)), jnp.float32)
    mobility = jnp.clip(jnp.exp(math.log(3.0) - 2.3025851 * jax.random.uniform(seeds[1], (NZ, NX, NY), jnp.float32) ** steps_of(seeds[1], (NZ, NX, NY), ((1, 32), (2, 8)), -0.2, 0.2)), 0.3, 3.0)
    block_x = normal_values(seeds[2], (NZ, NX, CX), CX ** -0.5, 0.75, ((1, 32),), jnp.float32)
    spike_x = normal_values(seeds[3], (NZ, NX, 4), 0.5, 3.0, ((1, 32),), jnp.float32)
    reduced_x = normal_values(seeds[4], (NZ, RX, RX), RX ** -0.5, 0.5, (), jnp.float32)
    block_y = normal_values(seeds[5], (NZ, NY, CY), CY ** -0.5, 0.5, ((1, 8),), jnp.float32)
    spike_y = normal_values(seeds[6], (NZ, NY, 4), 0.5, 3.0, ((1, 8),), jnp.float32)
    reduced_y = normal_values(seeds[7], (NZ, RY, RY), RY ** -0.5, 1.0, (), jnp.float32)
    return {"conc": conc, "mobility": mobility, "block_x": block_x, "spike_x": spike_x, "reduced_x": reduced_x, "block_y": block_y, "spike_y": spike_y, "reduced_y": reduced_y}


HIGH = lax.Precision.HIGHEST


def explicit_part(conc, mobility):
    def roll_sum(field):
        return (jnp.roll(field, 1, 1) + jnp.roll(field, -1, 1)
                + jnp.roll(field, 1, 2) + jnp.roll(field, -1, 2))
    lap = roll_sum(conc) - 4.0 * conc
    mu = conc * conc * conc - conc - 1.0 * lap
    sq = conc * conc
    mob = mobility * (0.25 + sq) / (1.0 + sq)
    div = jnp.zeros_like(conc)
    for shift, axis in ((1, 1), (-1, 1), (1, 2), (-1, 2)):
        div = div + 0.5 * (jnp.roll(mob, shift, axis) + mob) * (jnp.roll(mu, shift, axis) - mu)
    return conc + 0.02 * div


def solve_lines_x(field, block_x, spike_x, reduced_x):
    planes, total, cols = field.shape
    width = block_x.shape[2]
    count = total // width
    mats = block_x.reshape(planes, count, width, width)
    lin = jnp.einsum('zpij,zpjn->zpin', mats, field.reshape(planes, count, width, cols), precision=HIGH)
    rims = jnp.concatenate([lin[:, :, 0:2], lin[:, :, width - 2:]], axis=2).reshape(planes, 4 * count, cols)
    unknowns = jnp.einsum('zrk,zkn->zrn', reduced_x, rims, precision=HIGH).reshape(planes, count, 4, cols)
    coupled = jnp.concatenate([jnp.roll(unknowns, 1, 1)[:, :, 2:4], jnp.roll(unknowns, -1, 1)[:, :, 0:2]], axis=2)
    spikes = spike_x.reshape(planes, count, width, 4)
    out = lin - jnp.einsum('zpik,zpkn->zpin', spikes, coupled, precision=HIGH)
    return out.reshape(planes, total, cols)


def solve_lines_y(field, block_y, spike_y, reduced_y):
    planes, rows, total = field.shape
    width = block_y.shape[2]
    count = total // width
    mats = block_y.reshape(planes, count, width, width)
    lin = jnp.einsum('zqij,zxqj->zxqi', mats, field.reshape(planes, rows, count, width), precision=HIGH)
    rims = jnp.concatenate([lin[..., 0:2], lin[..., width - 2:]], axis=3).reshape(planes, rows, 4 * count)
    unknowns = jnp.einsum('zrk,zxk->zxr', reduced_y, rims, precision=HIGH).reshape(planes, rows, count, 4)
    coupled = jnp.concatenate([jnp.roll(unknowns, 1, 2)[..., 2:4], jnp.roll(unknowns, -1, 2)[..., 0:2]], axis=3)
    spikes = spike_y.reshape(planes, count, width, 4)
    out = lin - jnp.einsum('zqik,zxqk->zxqi', spikes, coupled, precision=HIGH)
    return out.reshape(planes, rows, total)


def reference(conc, mobility, block_x, spike_x, reduced_x, block_y, spike_y, reduced_y):
    rhs = explicit_part(conc, mobility)
    xsol = solve_lines_x(rhs, block_x, spike_x, reduced_x)
    return solve_lines_y(xsol, block_y, spike_y, reduced_y)
```

```python
import jax
import jax.numpy as jnp
from jax import lax
from jax.experimental import pallas as pl
from jax.experimental.pallas import tpu as pltpu
from jax.sharding import PartitionSpec as P

NZ, CX, CY = 32, 64, 128
STEP = 4
F32, BF16 = jnp.float32, jnp.bfloat16
CALL = pltpu.CompilerParams(vmem_limit_bytes=48 * 1024 * 1024)


def halves(a):
    hi = a.astype(BF16)
    return hi, (a - hi.astype(F32)).astype(BF16)


def dot3(a, b, dims):
    ah, al = halves(a)
    bh, bl = halves(b)
    one = lambda x, y: lax.dot_general(x, y, (dims, ((), ())), preferred_element_type=F32)
    return one(ah, bh) + (one(ah, bl) + one(al, bh))


def iota(shape, axis):
    return lax.broadcasted_iota(jnp.int32, shape, axis)


def roll(a, shift, axis):
    if isinstance(shift, int) and shift % a.shape[axis] == 0:
        return a
    if isinstance(shift, int):
        shift = shift % a.shape[axis]
    return pltpu.roll(a, shift, axis)


def potential(c, lap):
    return c * c * c - c - lap


def mobile(prefactor, c):
    sq = c * c
    return prefactor * (0.25 + sq) / (1.0 + sq)


def pack_kernel(c_ref, m_ref, ylo_ref, yhi_ref, xlo_ref, xhi_ref):
    lane = iota((CX, CY), 1)
    lo = jnp.zeros((CX, CY), F32)
    hi = jnp.zeros((CX, CY), F32)
    for z in range(NZ):
        c = roll(c_ref[z], 4 * z, 1)
        m = roll(m_ref[z], 4 * z + 2, 1)
        a, b = (4 * z - 2) % CY, 4 * z
        lo = jnp.where((lane >= b) & (lane <= b + 1), c, lo)
        lo = jnp.where(lane == b + 2, m, lo)
        hi = jnp.where((lane >= a) & (lane <= a + 1), c, hi)
        hi = jnp.where(lane == b + 1, m, hi)
    ylo_ref[...] = lo
    yhi_ref[...] = hi
    xlo_ref[0:32] = c_ref[:, 0, :]
    xlo_ref[32:64] = c_ref[:, 1, :]
    xlo_ref[64:96] = m_ref[:, 0, :]
    xhi_ref[0:32] = c_ref[:, CX - 1, :]
    xhi_ref[32:64] = c_ref[:, CX - 2, :]
    xhi_ref[64:96] = m_ref[:, CX - 1, :]


def lines_kernel(c_ref, m_ref, bx_ref, own_lo, own_hi, ylo_ref, yhi_ref, yl_ref, yr_ref,
                 xl_ref, xr_ref, lin_ref, rim_ref, ch, fh, mul, mobl, mur, mobr):
    row = iota((CX, CY), 0)
    lane = iota((CX, CY), 1)
    pid = pl.program_id(0)

    @pl.when(pid == 0)
    def _():
        lo, hi, left, right = ylo_ref[...], yhi_ref[...], yl_ref[...], yr_ref[...]

        def around(a, k):
            up = jnp.where(row == 0, xl_ref[96 + k:97 + k], roll(a, 1, 0))
            down = jnp.where(row == CX - 1, xr_ref[96 + k:97 + k], roll(a, -1, 0))
            return up + down

        c0, c1, m0 = lo, roll(lo, -1, 1), roll(lo, -2, 1)
        cm1, cm2, mm1 = roll(left, 1, 1), roll(left, 2, 1), roll(left, -1, 1)
        mu0 = potential(c0, cm1 + c1 + around(lo, 0) - 4.0 * c0)
        mum1 = potential(cm1, cm2 + c0 + roll(around(left, 2), 1, 1) - 4.0 * cm1)
        flux_l = 0.5 * (mobile(mm1, cm1) + mobile(m0, c0)) * (mu0 - mum1)
        cn, cn1, mn = hi, roll(hi, 1, 1), roll(hi, -2, 1)
        cp, cp2, mp = roll(right, -1, 1), roll(right, -2, 1), roll(right, -3, 1)
        mun = potential(cn, cn1 + cp + around(hi, 1) - 4.0 * cn)
        mup = potential(cp, cn + cp2 + roll(around(right, 3), -1, 1) - 4.0 * cp)
        flux_r = 0.5 * (mobile(mp, cp) + mobile(mn, cn)) * (mup - mun)
        first = (lane & 3) == 0
        fh[...] = jnp.where(first, flux_l, flux_r)
        ch[...] = jnp.where(first, cm1, cp)

        sub, ln = iota((NZ, CY), 0), iota((NZ, CY), 1)

        def halo_row(x_ref, own, mu_out, mob_out):
            a = x_ref[0:32]
            west = jnp.sum(jnp.where(ln == ((4 * sub - 1) & 127), x_ref[98:99], 0.0), axis=1, keepdims=True)
            east = jnp.sum(jnp.where(ln == 4 * sub, x_ref[99:100], 0.0), axis=1, keepdims=True)
            lf = jnp.where(ln == 0, west, roll(a, 1, 1))
            rt = jnp.where(ln == CY - 1, east, roll(a, -1, 1))
            mu_out[...] = potential(a, x_ref[32:64] + own[0:32] + lf + rt - 4.0 * a)
            mob_out[...] = mobile(x_ref[64:96], a)

        halo_row(xl_ref, own_lo, mul, mobl)
        halo_row(xr_ref, own_hi, mur, mobr)

    for i in range(STEP):
        z = pid * STEP + i
        at = pl.ds(z, 1)
        turn = (CY - 4 * z) & (CY - 1)
        c = c_ref[i]
        hz = roll(ch[...], turn, 1)
        fz = roll(fh[...], turn, 1)
        up = jnp.where(row == 0, xl_ref[at], roll(c, 1, 0))
        down = jnp.where(row == CX - 1, xr_ref[at], roll(c, -1, 0))
        lf = jnp.where(lane == 0, hz, roll(c, 1, 1))
        rt = jnp.where(lane == CY - 1, hz, roll(c, -1, 1))
        mu = potential(c, up + down + lf + rt - 4.0 * c)
        mob = mobile(m_ref[i], c)
        mu_d = jnp.where(row == CX - 1, mur[at], roll(mu, -1, 0))
        mob_d = jnp.where(row == CX - 1, mobr[at], roll(mob, -1, 0))
        fx = 0.5 * (mob_d + mob) * (mu_d - mu)
        f0 = 0.5 * (mob[0:1] + mobl[at]) * (mu[0:1] - mul[at])
        fx_up = jnp.where(row == 0, f0, roll(fx, 1, 0))
        fy = 0.5 * (roll(mob, -1, 1) + mob) * (roll(mu, -1, 1) - mu)
        fy = jnp.where(lane == CY - 1, fz, fy)
        fy_lf = jnp.where(lane == 0, fz, roll(fy, 1, 1))
        rhs = c + 0.02 * ((fx - fx_up) + (fy - fy_lf))
        lin = dot3(bx_ref[i], rhs, ((1,), (0,)))
        lin_ref[i] = lin
        rim_ref[i, 0:2] = lin[0:2]
        rim_ref[i, 2:4] = lin[CX - 2:CX]


def reduced_kernel(r_ref, rim_ref, out_ref):
    r = r_ref[...]
    use = jnp.where((iota((4 * NZ, 4 * NZ), 0) & 3) < 2, roll(r, 2, 0), roll(r, -2, 0))
    out_ref[...] = dot3(use, rim_ref[...], ((1,), (0,)))


def middle_kernel(lin_ref, cx_ref, sx_ref, by_ref, y_ref, rim_ref):
    pid = pl.program_id(0)
    lane = iota((CX, CY), 1)

    @pl.when(pid == 0)
    def _():
        rim_ref[...] = jnp.zeros_like(rim_ref)

    acc = rim_ref[...]
    for i in range(STEP):
        z = pid * STEP + i
        v = lin_ref[i] - lax.dot_general(sx_ref[i], cx_ref[i], (((0,), (0,)), ((), ())),
                                         precision=lax.Precision.HIGHEST, preferred_element_type=F32)
        y = dot3(v, by_ref[i], ((1,), (1,)))
        y_ref[i] = y
        acc = jnp.where((lane >> 2) == z, roll(y, (4 * z + 2) & (CY - 1), 1), acc)
    rim_ref[...] = acc


def last_kernel(y_ref, g_ref, bd_ref, sy_ref, out_ref, cy):
    pid = pl.program_id(0)
    lane = iota((CX, CY), 1)

    @pl.when(pid == 0)
    def _():
        total = jnp.zeros((CX, CY), F32)
        for q in range(8):
            total = total + dot3(g_ref[q], bd_ref[q], ((1,), (0,)))
        cy[...] = total

    c = cy[...]
    for i in range(STEP):
        z = pid * STEP + i
        mine = jnp.where((lane >> 2) == z, c, 0.0)
        out_ref[i] = y_ref[i] - dot3(mine, sy_ref[...], ((1,), (0,)))


def planes(rows, cols):
    return pl.BlockSpec((STEP, rows, cols), lambda i: (i, 0, 0))


def whole(*shape):
    return pl.BlockSpec(shape, lambda i: (0,) * len(shape))


def shape(*dims):
    return jax.ShapeDtypeStruct(dims, F32)


def body(conc, mobility, block_x, spike_x, reduced_x, block_y, spike_y, reduced_y):
    nx, ny = lax.axis_size("gx"), lax.axis_size("gy")
    p, q = lax.axis_index("gx"), lax.axis_index("gy")
    ring = lambda n, s: [(i, (i + s) % n) for i in range(n)]
    grid = (NZ // STEP,)

    ylo, yhi, xlo, xhi = pl.pallas_call(
        pack_kernel,
        out_shape=(shape(CX, CY), shape(CX, CY), shape(96, CY), shape(96, CY)),
        compiler_params=CALL,
        name="pack",
    )(conc, mobility)
    yl = lax.ppermute(yhi, "gy", ring(ny, 1))
    yr = lax.ppermute(ylo, "gy", ring(ny, -1))
    pad = jnp.zeros((4, CY), F32)
    send_lo = jnp.concatenate([xlo, ylo[:1], yhi[:1], yl[:1], yr[:1], pad])
    send_hi = jnp.concatenate([xhi, ylo[-1:], yhi[-1:], yl[-1:], yr[-1:], pad])
    xl = lax.ppermute(send_hi, "gx", ring(nx, 1))
    xr = lax.ppermute(send_lo, "gx", ring(nx, -1))

    lin, rims = pl.pallas_call(
        lines_kernel,
        grid=grid,
        in_specs=[planes(CX, CY), planes(CX, CY), planes(CX, CX), whole(96, CY), whole(96, CY),
                  whole(CX, CY), whole(CX, CY), whole(CX, CY), whole(CX, CY), whole(104, CY), whole(104, CY)],
        out_specs=(planes(CX, CY), planes(4, CY)),
        out_shape=(shape(NZ, CX, CY), shape(NZ, 4, CY)),
        scratch_shapes=[pltpu.VMEM((CX, CY), F32)] * 2 + [pltpu.VMEM((NZ, CY), F32)] * 4,
        compiler_params=CALL,
        name="lines",
    )(conc, mobility, block_x, xlo, xhi, ylo, yhi, yl, yr, xl, xr)

    mine = lax.dynamic_index_in_dim(reduced_x, p, 0, keepdims=False)
    rims = lax.all_to_all(rims, "gx", 0, 0, tiled=True)
    solved = pl.pallas_call(
        reduced_kernel, out_shape=shape(4 * NZ, CY), compiler_params=CALL, name="reduced"
    )(mine, rims.reshape(4 * NZ, CY))
    cx = lax.all_to_all(solved.reshape(NZ, 4, CY), "gx", 0, 0, tiled=True)

    ylin, yrim = pl.pallas_call(
        middle_kernel,
        grid=grid,
        in_specs=[planes(CX, CY), planes(4, CY), planes(4, CX), planes(CY, CY)],
        out_specs=(planes(CX, CY), whole(CX, CY)),
        out_shape=(shape(NZ, CX, CY), shape(CX, CY)),
        compiler_params=CALL,
        name="middle",
    )(lin, cx, jnp.transpose(spike_x, (0, 2, 1)), block_y)

    picks = (4 * q + jnp.array([-2, -1, 4, 5], jnp.int32)) % (4 * ny)
    rows = jnp.take(reduced_y, picks, axis=1).reshape(NZ, 4, ny, 4)
    rows = jnp.roll(rows, 2, axis=3)
    blocks = jnp.transpose(rows, (2, 0, 3, 1))[:, :, :, None, :]
    same = jnp.eye(NZ, dtype=F32)[None, :, None, :, None]
    diag = (blocks * same).reshape(ny, 4 * NZ, 4 * NZ)

    yall = lax.all_to_all(jnp.broadcast_to(yrim[None], (ny, CX, CY)), "gy", 0, 0, tiled=True)
    return pl.pallas_call(
        last_kernel,
        grid=grid,
        in_specs=[planes(CX, CY), whole(ny, CX, CY), whole(ny, CY, CY), whole(4 * NZ, CY)],
        out_specs=planes(CX, CY),
        out_shape=shape(NZ, CX, CY),
        scratch_shapes=[pltpu.VMEM((CX, CY), F32)],
        compiler_params=CALL,
        name="last",
    )(ylin, yall, diag, jnp.transpose(spike_y, (0, 2, 1)).reshape(4 * NZ, CY))


def solution(mesh):
    in_specs = (
        P(None, "gx", "gy"),
        P(None, "gx", "gy"),
        P(None, "gx", None),
        P(None, "gx", None),
        P(),
        P(None, "gy", None),
        P(None, "gy", None),
        P(),
    )
    out_specs = P(None, "gx", "gy")
    return jax.shard_map(body, mesh=mesh, in_specs=in_specs, out_specs=out_specs, check_vma=False)
```

```python
import jax
import jax.numpy as jnp
from jax import lax
from jax.experimental import pallas as pl
from jax.experimental.pallas import tpu as pltpu
from jax.sharding import PartitionSpec as P

NZ, CX, CY = 32, 64, 128
STEP = 4
F32, BF16 = jnp.float32, jnp.bfloat16
CALL = pltpu.CompilerParams(vmem_limit_bytes=12 * 1024 * 1024)


def halves(a):
    hi = a.astype(BF16)
    return hi, (a - hi.astype(F32)).astype(BF16)


def dot3(a, b, dims):
    ah, al = halves(a)
    bh, bl = halves(b)
    one = lambda x, y: lax.dot_general(x, y, (dims, ((), ())), preferred_element_type=F32)
    return one(ah, bh) + (one(ah, bl) + one(al, bh))


def iota(shape, axis):
    return lax.broadcasted_iota(jnp.int32, shape, axis)


def roll(a, shift, axis):
    if isinstance(shift, int) and shift % a.shape[axis] == 0:
        return a
    if isinstance(shift, int):
        shift = shift % a.shape[axis]
    return pltpu.roll(a, shift, axis)


def potential(c, lap):
    return c * c * c - c - lap


def mobile(prefactor, c):
    sq = c * c
    return prefactor * (0.25 + sq) / (1.0 + sq)


def edge_kernel(c_ref, m_ref, xlo_ref, xhi_ref, ct, cb, mt, mb, sems):
    top, bottom = pl.ds(0, 8), pl.ds(CX - 8, 8)
    copies = [
        pltpu.make_async_copy(c_ref.at[:, top, :], ct, sems.at[0]),
        pltpu.make_async_copy(m_ref.at[:, top, :], mt, sems.at[1]),
        pltpu.make_async_copy(c_ref.at[:, bottom, :], cb, sems.at[2]),
        pltpu.make_async_copy(m_ref.at[:, bottom, :], mb, sems.at[3]),
    ]
    for copy in copies:
        copy.start()
    for copy in copies:
        copy.wait()
    xlo_ref[0:32] = ct[:, 0, :]
    xlo_ref[32:64] = ct[:, 1, :]
    xlo_ref[64:96] = mt[:, 0, :]
    xhi_ref[0:32] = cb[:, 7, :]
    xhi_ref[32:64] = cb[:, 6, :]
    xhi_ref[64:96] = mb[:, 7, :]


def pack_kernel(c_ref, m_ref, ylo_ref, yhi_ref):
    lane = iota((CX, CY), 1)
    lo = jnp.zeros((CX, CY), F32)
    hi = jnp.zeros((CX, CY), F32)
    for z in range(NZ):
        c = roll(c_ref[z], 4 * z, 1)
        m = roll(m_ref[z], 4 * z + 2, 1)
        a, b = (4 * z - 2) % CY, 4 * z
        lo = jnp.where((lane >= b) & (lane <= b + 1), c, lo)
        lo = jnp.where(lane == b + 2, m, lo)
        hi = jnp.where((lane >= a) & (lane <= a + 1), c, hi)
        hi = jnp.where(lane == b + 1, m, hi)
    ylo_ref[...] = lo
    yhi_ref[...] = hi


def corner_kernel(lo_ref, hi_ref, xl_ref, xr_ref, slo_ref, shi_ref):
    sub, lane = iota((NZ, CY), 0), iota((NZ, CY), 1)

    def across(column, at):
        return jnp.sum(jnp.where(lane == at, column, 0.0), axis=0, keepdims=True)

    pad = jnp.zeros((6, CY), F32)
    up, down = xl_ref[0:NZ], xr_ref[0:NZ]
    first, last = 4 * sub, (4 * sub - 1) & (CY - 1)
    slo_ref[0:CX] = lo_ref[...]
    slo_ref[CX:72] = jnp.concatenate([across(up[:, :1], first), across(down[:, :1], first), pad])
    shi_ref[0:CX] = hi_ref[...]
    shi_ref[CX:72] = jnp.concatenate([across(up[:, CY - 1:], last), across(down[:, CY - 1:], last), pad])


def piece(src, dst, sems, g):
    at = pl.ds(g * STEP, STEP)
    return pltpu.make_async_copy(src.at[at], dst.at[at], sems.at[g])


def lines_kernel(c_hbm, m_hbm, bx_hbm, own_lo, own_hi, slo_ref, shi_ref, yl_ref, yr_ref,
                 xl_ref, xr_ref, lin_hbm, rim_ref, c_ref, m_ref, bx_ref, lin_ref, ch, fh, mul, mobl, mur, mobr, sems):
    row = iota((CX, CY), 0)
    lane = iota((CX, CY), 1)
    moves = ((c_hbm, c_ref), (m_hbm, m_ref), (bx_hbm, bx_ref), (lin_ref, lin_hbm))
    for g in range(NZ // STEP):
        for k in range(3):
            piece(*moves[k], sems.at[k], g).start()

    def edges():
        lo, hi, left, right = slo_ref[0:CX], shi_ref[0:CX], yl_ref[0:CX], yr_ref[0:CX]

        def around(a, ref):
            up = jnp.where(row == 0, ref[CX:CX + 1], roll(a, 1, 0))
            down = jnp.where(row == CX - 1, ref[CX + 1:CX + 2], roll(a, -1, 0))
            return up + down

        c0, c1, m0 = lo, roll(lo, -1, 1), roll(lo, -2, 1)
        cm1, cm2, mm1 = roll(left, 1, 1), roll(left, 2, 1), roll(left, -1, 1)
        mu0 = potential(c0, cm1 + c1 + around(lo, slo_ref) - 4.0 * c0)
        mum1 = potential(cm1, cm2 + c0 + roll(around(left, yl_ref), 1, 1) - 4.0 * cm1)
        flux_l = 0.5 * (mobile(mm1, cm1) + mobile(m0, c0)) * (mu0 - mum1)
        cn, cn1, mn = hi, roll(hi, 1, 1), roll(hi, -2, 1)
        cp, cp2, mp = roll(right, -1, 1), roll(right, -2, 1), roll(right, -3, 1)
        mun = potential(cn, cn1 + cp + around(hi, shi_ref) - 4.0 * cn)
        mup = potential(cp, cn + cp2 + roll(around(right, yr_ref), -1, 1) - 4.0 * cp)
        flux_r = 0.5 * (mobile(mp, cp) + mobile(mn, cn)) * (mup - mun)
        first = (lane & 3) == 0
        fh[...] = jnp.where(first, flux_l, flux_r)
        ch[...] = jnp.where(first, cm1, cp)

        sub, ln = iota((NZ, CY), 0), iota((NZ, CY), 1)

        def halo_row(x_ref, own, k, mu_out, mob_out):
            a = x_ref[0:32]
            west = jnp.where(ln == ((4 * sub - 1) & (CY - 1)), yl_ref[CX + k:CX + k + 1], 0.0)
            east = jnp.where(ln == 4 * sub, yr_ref[CX + k:CX + k + 1], 0.0)
            lf = jnp.where(ln == 0, jnp.sum(west, axis=1, keepdims=True), roll(a, 1, 1))
            rt = jnp.where(ln == CY - 1, jnp.sum(east, axis=1, keepdims=True), roll(a, -1, 1))
            mu_out[...] = potential(a, x_ref[32:64] + own[0:32] + lf + rt - 4.0 * a)
            mob_out[...] = mobile(x_ref[64:96], a)

        halo_row(xl_ref, own_lo, 0, mul, mobl)
        halo_row(xr_ref, own_hi, 1, mur, mobr)

    edges()

    def step(g, carry):
        for k in range(3):
            piece(*moves[k], sems.at[k], g).wait()
        for i in range(STEP):
            plane(g * STEP + i)
        piece(*moves[3], sems.at[3], g).start()
        return carry

    def plane(z):
        at = pl.ds(z, 1)
        turn = (CY - 4 * z) & (CY - 1)
        c = c_ref[z]
        hz = roll(ch[...], turn, 1)
        fz = roll(fh[...], turn, 1)
        up = jnp.where(row == 0, xl_ref[at], roll(c, 1, 0))
        down = jnp.where(row == CX - 1, xr_ref[at], roll(c, -1, 0))
        lf = jnp.where(lane == 0, hz, roll(c, 1, 1))
        rt = jnp.where(lane == CY - 1, hz, roll(c, -1, 1))
        mu = potential(c, up + down + lf + rt - 4.0 * c)
        mob = mobile(m_ref[z], c)
        mu_d = jnp.where(row == CX - 1, mur[at], roll(mu, -1, 0))
        mob_d = jnp.where(row == CX - 1, mobr[at], roll(mob, -1, 0))
        fx = 0.5 * (mob_d + mob) * (mu_d - mu)
        f0 = 0.5 * (mob[0:1] + mobl[at]) * (mu[0:1] - mul[at])
        fx_up = jnp.where(row == 0, f0, roll(fx, 1, 0))
        fy = 0.5 * (roll(mob, -1, 1) + mob) * (roll(mu, -1, 1) - mu)
        fy = jnp.where(lane == CY - 1, fz, fy)
        fy_lf = jnp.where(lane == 0, fz, roll(fy, 1, 1))
        rhs = c + 0.02 * ((fx - fx_up) + (fy - fy_lf))
        lin = dot3(bx_ref[z], rhs, ((1,), (0,)))
        lin_ref[z] = lin
        rim_ref[z, 0:2] = lin[0:2]
        rim_ref[z, 2:4] = lin[CX - 2:CX]

    lax.fori_loop(0, NZ // STEP, step, 0)
    for g in range(NZ // STEP):
        piece(*moves[3], sems.at[3], g).wait()


def reduced_kernel(r_ref, rim_ref, out_ref):
    r = r_ref[...]
    use = jnp.where((iota((4 * NZ, 4 * NZ), 0) & 3) < 2, roll(r, 2, 0), roll(r, -2, 0))
    out_ref[...] = dot3(use, rim_ref[...], ((1,), (0,)))


def wide_kernel(lin_ref, byr_ref, rim_ref):
    lane = iota((CX, CY), 1)
    acc = jnp.zeros((CX, CY), F32)
    for g in range(NZ // STEP):
        part = lin_ref[STEP * g:STEP * (g + 1)].reshape(STEP * CX, CY)
        out = dot3(part, byr_ref[...], ((1,), (1,)))
        for i in range(STEP):
            acc = jnp.where((lane >> 2) == STEP * g + i, out[CX * i:CX * (i + 1)], acc)
    rim_ref[...] = acc


def diag_kernel(y_ref, hi_ref, lo_ref):
    n = 4 * NZ
    yh, yl = halves(y_ref[...])
    same = (iota((n, n), 0) >> 2) == (iota((n, n), 1) >> 2)
    col, ln = iota((32, n), 0), iota((32, n), 1)
    for q in range(8):
        pick = jnp.where(col == 4 * q + ((ln + 2) & 3), 1.0, 0.0).astype(BF16)
        for a, ref in ((yh, hi_ref), (yl, lo_ref)):
            full = jnp.dot(a, pick, preferred_element_type=F32)
            ref[q] = jnp.where(same, full, 0.0).astype(BF16)


def rims_kernel(wrim_ref, cx_ref, byr_ref, sx_ref, out_ref):
    n = 4 * NZ
    same = (iota((n, n), 0) >> 2) == (iota((n, n), 1) >> 2)
    mixed = jnp.where(same, dot3(cx_ref[...], byr_ref[...], ((1,), (1,))), 0.0)
    v = wrim_ref[...] - dot3(sx_ref[...], mixed, ((0,), (0,)))
    for q in range(8):
        out_ref[q] = v


def spread(packed, g):
    lane = iota((CX, CY), 1)
    return jnp.concatenate([jnp.where((lane >> 2) == STEP * g + i, packed, 0.0) for i in range(STEP)])


def couple_kernel(lin_hbm, by_hbm, cx_ref, sx_ref, u_hbm, lin, by, u, spikes, sems):
    for g in range(NZ // STEP):
        piece(lin_hbm, lin, sems.at[0], g).start()
        piece(by_hbm, by, sems.at[1], g).start()
    spikes[...] = jnp.transpose(sx_ref[...])

    def step(g, carry):
        fix = dot3(spread(spikes[...], g), cx_ref[...], ((1,), (0,)))
        piece(lin_hbm, lin, sems.at[0], g).wait()
        piece(by_hbm, by, sems.at[1], g).wait()
        for i in range(STEP):
            z = STEP * g + i
            v = lin[z] - fix[CX * i:CX * (i + 1)]
            u[z] = dot3(v, by[z], ((1,), (1,)))
        piece(u, u_hbm, sems.at[2], g).start()
        return carry

    lax.fori_loop(0, NZ // STEP, step, 0)
    for g in range(NZ // STEP):
        piece(u, u_hbm, sems.at[2], g).wait()


def last_kernel(u_hbm, g_ref, dh_ref, dl_ref, sy_ref, out_hbm, u, cy, sems):
    nt = lambda a, b: lax.dot_general(a, b, (((1,), (1,)), ((), ())), preferred_element_type=F32)
    for g in range(NZ // STEP):
        piece(u_hbm, u, sems.at[0], g).start()
    total = jnp.zeros((CX, CY), F32)
    for q in range(8):
        gh, gl = halves(g_ref[q])
        total = total + (nt(gh, dh_ref[q]) + (nt(gh, dl_ref[q]) + nt(gl, dh_ref[q])))
    cy[...] = total

    def step(g, carry):
        fix = dot3(spread(cy[...], g), sy_ref[...], ((1,), (0,)))
        piece(u_hbm, u, sems.at[0], g).wait()
        for i in range(STEP):
            z = STEP * g + i
            u[z] = u[z] - fix[CX * i:CX * (i + 1)]
        piece(u, out_hbm, sems.at[1], g).start()
        return carry

    lax.fori_loop(0, NZ // STEP, step, 0)
    for g in range(NZ // STEP):
        piece(u, out_hbm, sems.at[1], g).wait()


def shape(*dims):
    return jax.ShapeDtypeStruct(dims, F32)


def body(conc, mobility, block_x, spike_x, reduced_x, block_y, spike_y, reduced_y):
    nx, ny = lax.axis_size("gx"), lax.axis_size("gy")
    p, q = lax.axis_index("gx"), lax.axis_index("gy")
    ring = lambda n, s: [(i, (i + s) % n) for i in range(n)]
    hbm = lambda a: pltpu.with_memory_space_constraint(a, pltpu.HBM)

    any_space = pl.BlockSpec(memory_space=pl.ANY)
    slab = pltpu.VMEM((NZ, 8, CY), F32)
    xlo, xhi = pl.pallas_call(
        edge_kernel,
        in_specs=[any_space, any_space],
        out_shape=(shape(96, CY), shape(96, CY)),
        scratch_shapes=[slab] * 4 + [pltpu.SemaphoreType.DMA((4,))],
        compiler_params=CALL, name="edge",
    )(hbm(conc), hbm(mobility))
    xl = lax.ppermute(xhi, "gx", ring(nx, 1))
    xr = lax.ppermute(xlo, "gx", ring(nx, -1))
    ylo, yhi = pl.pallas_call(
        pack_kernel, out_shape=(shape(CX, CY), shape(CX, CY)), compiler_params=CALL, name="pack"
    )(conc, mobility)
    slo, shi = pl.pallas_call(
        corner_kernel, out_shape=(shape(72, CY), shape(72, CY)), compiler_params=CALL, name="corner"
    )(ylo, yhi, xl, xr)
    yl = lax.ppermute(shi, "gy", ring(ny, 1))
    yr = lax.ppermute(slo, "gy", ring(ny, -1))

    full = lambda *dims: pltpu.VMEM(dims, F32)
    groups = NZ // STEP
    big = pltpu.HBM((NZ, CX, CY), F32)
    lin, rims = pl.pallas_call(
        lines_kernel,
        in_specs=[any_space] * 3 + [pl.BlockSpec()] * 8,
        out_specs=(any_space, pl.BlockSpec()),
        out_shape=(big, shape(NZ, 4, CY)),
        scratch_shapes=[full(NZ, CX, CY), full(NZ, CX, CY), full(NZ, CX, CX), full(NZ, CX, CY)]
        + [full(CX, CY)] * 2 + [full(NZ, CY)] * 4 + [pltpu.SemaphoreType.DMA((4, groups))],
        compiler_params=CALL, name="lines",
    )(hbm(conc), hbm(mobility), hbm(block_x), xlo, xhi, slo, shi, yl, yr, xl, xr)

    lin, rims, block_y, reduced_y = lax.optimization_barrier((lin, rims, block_y, reduced_y))
    sx = jnp.transpose(spike_x, (0, 2, 1)).reshape(4 * NZ, CX)
    sy = jnp.transpose(spike_y, (0, 2, 1)).reshape(4 * NZ, CY)
    byr = jnp.concatenate([block_y[:, CY - 2:], block_y[:, :2]], axis=1).reshape(4 * NZ, CY)
    wrim = pl.pallas_call(wide_kernel, out_shape=shape(CX, CY), compiler_params=CALL, name="wide")(lin, byr)
    below = lax.dynamic_slice_in_dim(reduced_y, (4 * q - 2) % (4 * ny), 2, 1)
    above = lax.dynamic_slice_in_dim(reduced_y, (4 * q + 4) % (4 * ny), 2, 1)
    used = jnp.concatenate([below, above], axis=1).reshape(4 * NZ, 4 * ny)
    dh, dl = pl.pallas_call(
        diag_kernel,
        out_shape=(jax.ShapeDtypeStruct((ny, CY, CY), BF16),) * 2,
        compiler_params=CALL, name="diag",
    )(used)

    mine = lax.dynamic_index_in_dim(reduced_x, p, 0, keepdims=False)
    rims = lax.all_to_all(rims, "gx", 0, 0, tiled=True)
    rims, wrim, dh, dl, mine = lax.optimization_barrier((rims, wrim, dh, dl, mine))
    solved = pl.pallas_call(
        reduced_kernel, out_shape=shape(4 * NZ, CY), compiler_params=CALL, name="reduced"
    )(mine, rims.reshape(4 * NZ, CY))
    cx = lax.all_to_all(solved.reshape(NZ, 4, CY), "gx", 0, 0, tiled=True).reshape(4 * NZ, CY)

    yrim = pl.pallas_call(rims_kernel, out_shape=shape(ny, CX, CY), compiler_params=CALL, name="rims")(
        wrim, cx, byr, sx
    )
    yall = lax.all_to_all(yrim, "gy", 0, 0, tiled=True)
    u = pl.pallas_call(
        couple_kernel,
        in_specs=[any_space, any_space, pl.BlockSpec(), pl.BlockSpec()],
        out_specs=any_space,
        out_shape=big,
        scratch_shapes=[full(NZ, CX, CY), full(NZ, CY, CY), full(NZ, CX, CY), full(CX, CY),
                        pltpu.SemaphoreType.DMA((3, groups))],
        compiler_params=CALL, name="couple",
    )(hbm(lin), hbm(block_y), cx, sx)
    return pl.pallas_call(
        last_kernel,
        in_specs=[any_space] + [pl.BlockSpec()] * 4,
        out_specs=any_space,
        out_shape=big,
        scratch_shapes=[full(NZ, CX, CY), full(CX, CY), pltpu.SemaphoreType.DMA((2, groups))],
        compiler_params=CALL, name="last",
    )(hbm(u), yall, dh, dl, sy)


def solution(mesh):
    in_specs = (
        P(None, "gx", "gy"),
        P(None, "gx", "gy"),
        P(None, "gx", None),
        P(None, "gx", None),
        P(),
        P(None, "gy", None),
        P(None, "gy", None),
        P(),
    )
    out_specs = P(None, "gx", "gy")
    return jax.shard_map(body, mesh=mesh, in_specs=in_specs, out_specs=out_specs, check_vma=False)
```

```python
import jax
import jax.numpy as jnp
from jax import lax
from jax.experimental import pallas as pl
from jax.experimental.pallas import tpu as pltpu
from jax.sharding import PartitionSpec as P

NZ, CX, CY = 32, 64, 128
STEP = 4
F32, BF16 = jnp.float32, jnp.bfloat16
CALL = pltpu.CompilerParams(vmem_limit_bytes=12 * 1024 * 1024)


def halves(a):
    hi = a.astype(BF16)
    return hi, (a - hi.astype(F32)).astype(BF16)


def dot3(a, b, dims):
    ah, al = halves(a)
    bh, bl = halves(b)
    one = lambda x, y: lax.dot_general(x, y, (dims, ((), ())), preferred_element_type=F32)
    return one(ah, bh) + (one(ah, bl) + one(al, bh))


def iota(shape, axis):
    return lax.broadcasted_iota(jnp.int32, shape, axis)


def roll(a, shift, axis):
    if isinstance(shift, int) and shift % a.shape[axis] == 0:
        return a
    if isinstance(shift, int):
        shift = shift % a.shape[axis]
    return pltpu.roll(a, shift, axis)


def potential(c, lap):
    return c * c * c - c - lap


def mobile(prefactor, c):
    sq = c * c
    return prefactor * (0.25 + sq) / (1.0 + sq)


def odd_at(axis):
    return (lax.axis_index(axis) & 1) == 1


def edge_kernel(c_ref, m_ref, first_ref, second_ref, ct, cb, mt, mb, sems):
    top, bottom = pl.ds(0, 8), pl.ds(CX - 8, 8)
    copies = [
        pltpu.make_async_copy(c_ref.at[:, top, :], ct, sems.at[0]),
        pltpu.make_async_copy(m_ref.at[:, top, :], mt, sems.at[1]),
        pltpu.make_async_copy(c_ref.at[:, bottom, :], cb, sems.at[2]),
        pltpu.make_async_copy(m_ref.at[:, bottom, :], mb, sems.at[3]),
    ]
    for copy in copies:
        copy.start()
    for copy in copies:
        copy.wait()
    odd = odd_at("gx")
    rows = ((ct[:, 0, :], cb[:, 7, :]), (ct[:, 1, :], cb[:, 6, :]), (mt[:, 0, :], mb[:, 7, :]))
    for k, (lo, hi) in enumerate(rows):
        first_ref[NZ * k:NZ * (k + 1)] = jnp.where(odd, lo, hi)
        second_ref[NZ * k:NZ * (k + 1)] = jnp.where(odd, hi, lo)


def pack_kernel(c_ref, m_ref, first_ref, second_ref):
    lane = iota((CX, CY), 1)
    lo = jnp.zeros((CX, CY), F32)
    hi = jnp.zeros((CX, CY), F32)
    for z in range(NZ):
        c = roll(c_ref[z], 4 * z, 1)
        m = roll(m_ref[z], 4 * z + 2, 1)
        a, b = (4 * z - 2) % CY, 4 * z
        lo = jnp.where((lane >= b) & (lane <= b + 1), c, lo)
        lo = jnp.where(lane == b + 2, m, lo)
        hi = jnp.where((lane >= a) & (lane <= a + 1), c, hi)
        hi = jnp.where(lane == b + 1, m, hi)
    odd = odd_at("gy")
    first_ref[...] = jnp.where(odd, lo, hi)
    second_ref[...] = jnp.where(odd, hi, lo)


def corner_kernel(side0_ref, side1_ref, got0_ref, got1_ref, first_ref, second_ref):
    sub, lane = iota((NZ, CY), 0), iota((NZ, CY), 1)
    odd_x, odd_y = odd_at("gx"), odd_at("gy")
    got0, got1 = got0_ref[0:NZ], got1_ref[0:NZ]
    up, down = jnp.where(odd_x, got0, got1), jnp.where(odd_x, got1, got0)
    pad = jnp.zeros((6, CY), F32)

    def rows(k, at):
        pick = lambda a: jnp.sum(jnp.where(lane == at, a[:, k:k + 1], 0.0), axis=0, keepdims=True)
        return jnp.concatenate([pick(up), pick(down), pad])

    lo, hi = rows(0, 4 * sub), rows(CY - 1, (4 * sub - 1) & (CY - 1))
    first_ref[0:CX] = side0_ref[...]
    second_ref[0:CX] = side1_ref[...]
    first_ref[CX:72] = jnp.where(odd_y, lo, hi)
    second_ref[CX:72] = jnp.where(odd_y, hi, lo)


def piece(src, dst, sems, g):
    at = pl.ds(g * STEP, STEP)
    return pltpu.make_async_copy(src.at[at], dst.at[at], sems.at[g])


def lines_kernel(c_hbm, m_hbm, bx_hbm, own0_ref, own1_ref, send0_ref, send1_ref, side0_ref, side1_ref, got0_ref,
                 got1_ref, lin_hbm, rim_ref, c_ref, m_ref, bx_ref, lin_ref, ch, fh, mul, mobl, mur, mobr, slo_ref,
                 shi_ref, yl_ref, yr_ref, xl_ref, xr_ref, sems):
    row = iota((CX, CY), 0)
    lane = iota((CX, CY), 1)
    loads = ((c_hbm, c_ref), (m_hbm, m_ref), (bx_hbm, bx_ref))
    for g in range(NZ // STEP):
        for k, (src, dst) in enumerate(loads):
            piece(src, dst, sems.at[k], g).start()
    odd_x, odd_y = odd_at("gx"), odd_at("gy")

    def edges():
        slo_ref[...] = jnp.where(odd_y, send0_ref[...], send1_ref[...])
        shi_ref[...] = jnp.where(odd_y, send1_ref[...], send0_ref[...])
        yl_ref[...] = jnp.where(odd_y, side0_ref[...], side1_ref[...])
        yr_ref[...] = jnp.where(odd_y, side1_ref[...], side0_ref[...])
        xl_ref[...] = jnp.where(odd_x, got0_ref[...], got1_ref[...])
        xr_ref[...] = jnp.where(odd_x, got1_ref[...], got0_ref[...])
        own_lo = jnp.where(odd_x, own0_ref[0:NZ], own1_ref[0:NZ])
        own_hi = jnp.where(odd_x, own1_ref[0:NZ], own0_ref[0:NZ])
        lo, hi, left, right = slo_ref[0:CX], shi_ref[0:CX], yl_ref[0:CX], yr_ref[0:CX]

        def around(a, ref):
            up = jnp.where(row == 0, ref[CX:CX + 1], roll(a, 1, 0))
            down = jnp.where(row == CX - 1, ref[CX + 1:CX + 2], roll(a, -1, 0))
            return up + down

        c0, c1, m0 = lo, roll(lo, -1, 1), roll(lo, -2, 1)
        cm1, cm2, mm1 = roll(left, 1, 1), roll(left, 2, 1), roll(left, -1, 1)
        mu0 = potential(c0, cm1 + c1 + around(lo, slo_ref) - 4.0 * c0)
        mum1 = potential(cm1, cm2 + c0 + roll(around(left, yl_ref), 1, 1) - 4.0 * cm1)
        flux_l = 0.5 * (mobile(mm1, cm1) + mobile(m0, c0)) * (mu0 - mum1)
        cn, cn1, mn = hi, roll(hi, 1, 1), roll(hi, -2, 1)
        cp, cp2, mp = roll(right, -1, 1), roll(right, -2, 1), roll(right, -3, 1)
        mun = potential(cn, cn1 + cp + around(hi, shi_ref) - 4.0 * cn)
        mup = potential(cp, cn + cp2 + roll(around(right, yr_ref), -1, 1) - 4.0 * cp)
        flux_r = 0.5 * (mobile(mp, cp) + mobile(mn, cn)) * (mup - mun)
        first = (lane & 3) == 0
        fh[...] = jnp.where(first, flux_l, flux_r)
        ch[...] = jnp.where(first, cm1, cp)

        sub, ln = iota((NZ, CY), 0), iota((NZ, CY), 1)

        def halo_row(x_ref, own, k, mu_out, mob_out):
            a = x_ref[0:32]
            west = jnp.where(ln == ((4 * sub - 1) & (CY - 1)), yl_ref[CX + k:CX + k + 1], 0.0)
            east = jnp.where(ln == 4 * sub, yr_ref[CX + k:CX + k + 1], 0.0)
            lf = jnp.where(ln == 0, jnp.sum(west, axis=1, keepdims=True), roll(a, 1, 1))
            rt = jnp.where(ln == CY - 1, jnp.sum(east, axis=1, keepdims=True), roll(a, -1, 1))
            mu_out[...] = potential(a, x_ref[32:64] + own + lf + rt - 4.0 * a)
            mob_out[...] = mobile(x_ref[64:96], a)

        halo_row(xl_ref, own_lo, 0, mul, mobl)
        halo_row(xr_ref, own_hi, 1, mur, mobr)

    edges()

    def step(g, carry):
        for k, (src, dst) in enumerate(loads):
            piece(src, dst, sems.at[k], g).wait()
        for i in range(STEP):
            plane(g * STEP + i)
        piece(lin_ref, lin_hbm, sems.at[3], g).start()
        return carry

    def plane(z):
        at = pl.ds(z, 1)
        turn = (CY - 4 * z) & (CY - 1)
        c = c_ref[z]
        hz = roll(ch[...], turn, 1)
        fz = roll(fh[...], turn, 1)
        up = jnp.where(row == 0, xl_ref[at], roll(c, 1, 0))
        down = jnp.where(row == CX - 1, xr_ref[at], roll(c, -1, 0))
        lf = jnp.where(lane == 0, hz, roll(c, 1, 1))
        rt = jnp.where(lane == CY - 1, hz, roll(c, -1, 1))
        mu = potential(c, up + down + lf + rt - 4.0 * c)
        mob = mobile(m_ref[z], c)
        mu_d = jnp.where(row == CX - 1, mur[at], roll(mu, -1, 0))
        mob_d = jnp.where(row == CX - 1, mobr[at], roll(mob, -1, 0))
        fx = 0.5 * (mob_d + mob) * (mu_d - mu)
        f0 = 0.5 * (mob[0:1] + mobl[at]) * (mu[0:1] - mul[at])
        fx_up = jnp.where(row == 0, f0, roll(fx, 1, 0))
        fy = 0.5 * (roll(mob, -1, 1) + mob) * (roll(mu, -1, 1) - mu)
        fy = jnp.where(lane == CY - 1, fz, fy)
        fy_lf = jnp.where(lane == 0, fz, roll(fy, 1, 1))
        rhs = c + 0.02 * ((fx - fx_up) + (fy - fy_lf))
        lin = dot3(bx_ref[z], rhs, ((1,), (0,)))
        lin_ref[z] = lin
        rim_ref[z, 0:2] = lin[0:2]
        rim_ref[z, 2:4] = lin[CX - 2:CX]

    lax.fori_loop(0, NZ // STEP, step, 0)
    for g in range(NZ // STEP):
        piece(lin_ref, lin_hbm, sems.at[3], g).wait()


def reduced_kernel(r_ref, rim_ref, out_ref):
    r = r_ref[...]
    use = jnp.where((iota((4 * NZ, 4 * NZ), 0) & 3) < 2, roll(r, 2, 0), roll(r, -2, 0))
    out_ref[...] = dot3(use, rim_ref[...], ((1,), (0,)))


def wide_kernel(lin_hbm, by_hbm, rim_ref, byr_ref, lin, low, high, sems):
    ends = [
        pltpu.make_async_copy(by_hbm.at[:, pl.ds(0, 8), :], low, sems.at[NZ // STEP]),
        pltpu.make_async_copy(by_hbm.at[:, pl.ds(CY - 8, 8), :], high, sems.at[NZ // STEP + 1]),
    ]
    for copy in ends:
        copy.start()
    for g in range(NZ // STEP):
        piece(lin_hbm, lin, sems, g).start()
    for copy in ends:
        copy.wait()
    for k in range(4):
        byr_ref[pl.ds(k, NZ, stride=4), :] = high[:, 6 + k, :] if k < 2 else low[:, k - 2, :]
    lane = iota((CX, CY), 1)
    acc = jnp.zeros((CX, CY), F32)
    for g in range(NZ // STEP):
        piece(lin_hbm, lin, sems, g).wait()
        part = lin[STEP * g:STEP * (g + 1)].reshape(STEP * CX, CY)
        out = dot3(part, byr_ref[...], ((1,), (1,)))
        for i in range(STEP):
            acc = jnp.where((lane >> 2) == STEP * g + i, out[CX * i:CX * (i + 1)], acc)
    rim_ref[...] = acc


def diag_kernel(y_ref, hi_ref, lo_ref):
    n = 4 * NZ
    r, col = iota((n, 32 * NZ), 0), iota((n, 32 * NZ), 1)
    k, q = r & 3, lax.axis_index("gy")
    used = (r >> 2) * 32 + ((4 * q + k + jnp.where(k < 2, -2, 2)) & 31)
    take = jnp.where(col == used, 1.0, 0.0).astype(BF16)
    same = (iota((n, n), 0) >> 2) == (iota((n, n), 1) >> 2)
    col, ln = iota((32, n), 0), iota((32, n), 1)
    for half, ref in zip(halves(y_ref[...]), (hi_ref, lo_ref)):
        mine = jnp.dot(take, half, preferred_element_type=F32).astype(BF16)
        for p in range(8):
            pick = jnp.where(col == 4 * p + ((ln + 2) & 3), 1.0, 0.0).astype(BF16)
            full = jnp.dot(mine, pick, preferred_element_type=F32)
            ref[:, n * p:n * (p + 1)] = jnp.where(same, full, 0.0).astype(BF16)


def rims_kernel(wrim_ref, cx_ref, byr_ref, sx_ref, out_ref):
    n = 4 * NZ
    same = (iota((n, n), 0) >> 2) == (iota((n, n), 1) >> 2)
    mixed = jnp.where(same, dot3(cx_ref[...], byr_ref[...], ((1,), (1,))), 0.0)
    v = wrim_ref[...] - dot3(sx_ref[...], mixed, ((0,), (0,)))
    for q in range(8):
        out_ref[q] = v


def spread(packed, g):
    lane = iota((CX, CY), 1)
    return jnp.concatenate([jnp.where((lane >> 2) == STEP * g + i, packed, 0.0) for i in range(STEP)])


def couple_kernel(lin_hbm, by_hbm, cx_ref, sx_ref, u_hbm, lin, by, u, spikes, sems):
    for g in range(NZ // STEP):
        piece(lin_hbm, lin, sems.at[0], g).start()
        piece(by_hbm, by, sems.at[1], g).start()
    spikes[...] = jnp.transpose(sx_ref[...])

    def step(g, carry):
        fix = dot3(spread(spikes[...], g), cx_ref[...], ((1,), (0,)))
        piece(lin_hbm, lin, sems.at[0], g).wait()
        piece(by_hbm, by, sems.at[1], g).wait()
        for i in range(STEP):
            z = STEP * g + i
            v = lin[z] - fix[CX * i:CX * (i + 1)]
            u[z] = dot3(v, by[z], ((1,), (1,)))
        piece(u, u_hbm, sems.at[2], g).start()
        return carry

    lax.fori_loop(0, NZ // STEP, step, 0)
    for g in range(NZ // STEP):
        piece(u, u_hbm, sems.at[2], g).wait()


def last_kernel(u_hbm, g_ref, dh_ref, dl_ref, sy_ref, out_hbm, u, cy, sems):
    nt = lambda a, b: lax.dot_general(a, b, (((1,), (1,)), ((), ())), preferred_element_type=F32)
    for g in range(NZ // STEP):
        piece(u_hbm, u, sems.at[0], g).start()
    gh, gl = halves(jnp.concatenate([g_ref[q] for q in range(8)], axis=1))
    cy[...] = nt(gh, dh_ref[...]) + (nt(gh, dl_ref[...]) + nt(gl, dh_ref[...]))

    def step(g, carry):
        fix = dot3(spread(cy[...], g), sy_ref[...], ((1,), (0,)))
        piece(u_hbm, u, sems.at[0], g).wait()
        for i in range(STEP):
            z = STEP * g + i
            u[z] = u[z] - fix[CX * i:CX * (i + 1)]
        piece(u, out_hbm, sems.at[1], g).start()
        return carry

    lax.fori_loop(0, NZ // STEP, step, 0)
    for g in range(NZ // STEP):
        piece(u, out_hbm, sems.at[1], g).wait()


def shape(*dims):
    return jax.ShapeDtypeStruct(dims, F32)


def body(conc, mobility, block_x, spike_x, reduced_x, block_y, spike_y, reduced_y):
    nx, ny = lax.axis_size("gx"), lax.axis_size("gy")
    p = lax.axis_index("gx")
    hbm = lambda a: pltpu.with_memory_space_constraint(a, pltpu.HBM)
    any_space = pl.BlockSpec(memory_space=pl.ANY)
    here = pl.BlockSpec()
    full = lambda *dims: pltpu.VMEM(dims, F32)
    groups = NZ // STEP
    big, big_hbm = shape(NZ, CX, CY), pltpu.HBM((NZ, CX, CY), F32)

    def pairs(n, start):
        ends = [(i % n, (i + 1) % n) for i in range(start, start + n, 2)]
        return ends + [(b, a) for a, b in ends]

    def swap(first, second, axis, n):
        return lax.ppermute(first, axis, pairs(n, 0)), lax.ppermute(second, axis, pairs(n, 1))

    own0, own1 = pl.pallas_call(
        edge_kernel,
        in_specs=[any_space, any_space],
        out_shape=(shape(3 * NZ, CY), shape(3 * NZ, CY)),
        scratch_shapes=[full(NZ, 8, CY)] * 4 + [pltpu.SemaphoreType.DMA((4,))],
        compiler_params=CALL, name="edge",
    )(hbm(conc), hbm(mobility))
    got0, got1 = swap(own0, own1, "gx", nx)
    side = pl.pallas_call(
        pack_kernel, out_shape=(shape(CX, CY),) * 2, compiler_params=CALL, name="pack"
    )(conc, mobility)
    send0, send1 = pl.pallas_call(
        corner_kernel, out_shape=(shape(72, CY),) * 2, compiler_params=CALL, name="corner"
    )(*side, got0, got1)
    side0, side1 = swap(send0, send1, "gy", ny)

    lin, rims = pl.pallas_call(
        lines_kernel,
        in_specs=[any_space] * 3 + [here] * 8,
        out_specs=(any_space, here),
        out_shape=(big_hbm, shape(NZ, 4, CY)),
        scratch_shapes=[full(NZ, CX, CY), full(NZ, CX, CY), full(NZ, CX, CX), full(NZ, CX, CY)]
        + [full(CX, CY)] * 2 + [full(NZ, CY)] * 4 + [full(72, CY)] * 4 + [full(3 * NZ, CY)] * 2
        + [pltpu.SemaphoreType.DMA((4, groups))],
        compiler_params=CALL, name="lines",
    )(hbm(conc), hbm(mobility), hbm(block_x), own0, own1, send0, send1, side0, side1, got0, got1)

    lin, rims, block_y, reduced_y = lax.optimization_barrier((lin, rims, block_y, reduced_y))
    sx = jnp.transpose(spike_x, (0, 2, 1)).reshape(4 * NZ, CX)
    sy = jnp.transpose(spike_y, (0, 2, 1)).reshape(4 * NZ, CY)
    wrim, byr = pl.pallas_call(
        wide_kernel,
        in_specs=[any_space] * 2,
        out_shape=(shape(CX, CY), shape(4 * NZ, CY)),
        scratch_shapes=[full(NZ, CX, CY)] + [full(NZ, 8, CY)] * 2 + [pltpu.SemaphoreType.DMA((groups + 2,))],
        compiler_params=CALL, name="wide",
    )(hbm(lin), hbm(block_y))
    dh, dl = pl.pallas_call(
        diag_kernel,
        out_shape=(jax.ShapeDtypeStruct((CY, ny * CY), BF16),) * 2,
        compiler_params=CALL, name="diag",
    )(reduced_y.reshape(NZ * 4 * ny, 4 * ny))

    mine = lax.dynamic_index_in_dim(reduced_x, p, 0, keepdims=False)
    rims = lax.all_to_all(rims, "gx", 0, 0, tiled=True)
    rims, wrim, dh, dl, mine = lax.optimization_barrier((rims, wrim, dh, dl, mine))
    solved = pl.pallas_call(
        reduced_kernel, out_shape=shape(4 * NZ, CY), compiler_params=CALL, name="reduced"
    )(mine, rims.reshape(4 * NZ, CY))
    cx = lax.all_to_all(solved.reshape(NZ, 4, CY), "gx", 0, 0, tiled=True).reshape(4 * NZ, CY)

    yrim = pl.pallas_call(rims_kernel, out_shape=shape(ny, CX, CY), compiler_params=CALL, name="rims")(
        wrim, cx, byr, sx
    )
    yall = lax.all_to_all(yrim, "gy", 0, 0, tiled=True)
    u = pl.pallas_call(
        couple_kernel,
        in_specs=[any_space, any_space, here, here],
        out_specs=any_space,
        out_shape=big_hbm,
        scratch_shapes=[full(NZ, CX, CY), full(NZ, CY, CY), full(NZ, CX, CY), full(CX, CY),
                        pltpu.SemaphoreType.DMA((3, groups))],
        compiler_params=CALL, name="couple",
    )(hbm(lin), hbm(block_y), cx, sx)
    return pl.pallas_call(
        last_kernel,
        in_specs=[any_space] + [here] * 4,
        out_specs=any_space,
        out_shape=big_hbm,
        scratch_shapes=[full(NZ, CX, CY), full(CX, CY), pltpu.SemaphoreType.DMA((2, groups))],
        compiler_params=CALL, name="last",
    )(hbm(u), yall, dh, dl, sy)


def solution(mesh):
    in_specs = (
        P(None, "gx", "gy"),
        P(None, "gx", "gy"),
        P(None, "gx", None),
        P(None, "gx", None),
        P(),
        P(None, "gy", None),
        P(None, "gy", None),
        P(),
    )
    out_specs = P(None, "gx", "gy")
    return jax.shard_map(body, mesh=mesh, in_specs=in_specs, out_specs=out_specs, check_vma=False)
```

```python
import jax
import jax.numpy as jnp
from jax import lax
from jax.experimental import pallas as pl
from jax.experimental.pallas import tpu as pltpu
from jax.sharding import PartitionSpec as P

NZ, CX, CY = 32, 64, 128
STEP = 8
F32, BF16 = jnp.float32, jnp.bfloat16
CALL = pltpu.CompilerParams(vmem_limit_bytes=12 * 1024 * 1024)


def halves(a):
    hi = a.astype(BF16)
    return hi, (a - hi.astype(F32)).astype(BF16)


def dot3(a, b, dims):
    ah, al = halves(a)
    bh, bl = halves(b)
    one = lambda x, y: lax.dot_general(x, y, (dims, ((), ())), preferred_element_type=F32)
    return one(ah, bh) + (one(ah, bl) + one(al, bh))


def iota(shape, axis):
    return lax.broadcasted_iota(jnp.int32, shape, axis)


def roll(a, shift, axis):
    if isinstance(shift, int) and shift % a.shape[axis] == 0:
        return a
    if isinstance(shift, int):
        shift = shift % a.shape[axis]
    return pltpu.roll(a, shift, axis)


def potential(c, lap):
    return c * c * c - c - lap


def mobile(prefactor, c):
    sq = c * c
    return prefactor * (0.25 + sq) / (1.0 + sq)


def odd_at(axis):
    return (lax.axis_index(axis) & 1) == 1


def edge_kernel(c_ref, m_ref, first_ref, second_ref, ct, cb, mt, mb, sems):
    top, bottom = pl.ds(0, 8), pl.ds(CX - 8, 8)
    copies = [
        pltpu.make_async_copy(c_ref.at[:, top, :], ct, sems.at[0]),
        pltpu.make_async_copy(m_ref.at[:, top, :], mt, sems.at[1]),
        pltpu.make_async_copy(c_ref.at[:, bottom, :], cb, sems.at[2]),
        pltpu.make_async_copy(m_ref.at[:, bottom, :], mb, sems.at[3]),
    ]
    for copy in copies:
        copy.start()
    for copy in copies:
        copy.wait()
    odd = odd_at("gx")
    rows = ((ct[:, 0, :], cb[:, 7, :]), (ct[:, 1, :], cb[:, 6, :]), (mt[:, 0, :], mb[:, 7, :]))
    for k, (lo, hi) in enumerate(rows):
        first_ref[NZ * k:NZ * (k + 1)] = jnp.where(odd, lo, hi)
        second_ref[NZ * k:NZ * (k + 1)] = jnp.where(odd, hi, lo)


def pack_kernel(c_ref, m_ref, first_ref, second_ref, mu_hbm, mob_hbm, mu_ref, mob_ref, sems):
    row, lane = iota((CX, CY), 0), iota((CX, CY), 1)
    lo = jnp.zeros((CX, CY), F32)
    hi = jnp.zeros((CX, CY), F32)
    for z in range(NZ):
        c = roll(c_ref[z], 4 * z, 1)
        m = roll(m_ref[z], 4 * z + 2, 1)
        a, b = (4 * z - 2) % CY, 4 * z
        lo = jnp.where((lane >= b) & (lane <= b + 1), c, lo)
        lo = jnp.where(lane == b + 2, m, lo)
        hi = jnp.where((lane >= a) & (lane <= a + 1), c, hi)
        hi = jnp.where(lane == b + 1, m, hi)
    odd = odd_at("gy")
    first_ref[...] = jnp.where(odd, lo, hi)
    second_ref[...] = jnp.where(odd, hi, lo)

    def step(g, carry):
        for i in range(STEP):
            z = g * STEP + i
            c = c_ref[z]
            up = jnp.where(row == 0, 0.0, roll(c, 1, 0))
            down = jnp.where(row == CX - 1, 0.0, roll(c, -1, 0))
            lf = jnp.where(lane == 0, 0.0, roll(c, 1, 1))
            rt = jnp.where(lane == CY - 1, 0.0, roll(c, -1, 1))
            mu_ref[z] = potential(c, up + down + lf + rt - 4.0 * c)
            mob_ref[z] = mobile(m_ref[z], c)
        piece(mu_ref, mu_hbm, sems.at[0], g).start()
        piece(mob_ref, mob_hbm, sems.at[1], g).start()
        return carry

    lax.fori_loop(0, NZ // STEP, step, 0)
    for g in range(NZ // STEP):
        piece(mu_ref, mu_hbm, sems.at[0], g).wait()
        piece(mob_ref, mob_hbm, sems.at[1], g).wait()


def corner_kernel(side0_ref, side1_ref, got0_ref, got1_ref, first_ref, second_ref):
    sub, lane = iota((NZ, CY), 0), iota((NZ, CY), 1)
    odd_x, odd_y = odd_at("gx"), odd_at("gy")
    got0, got1 = got0_ref[0:NZ], got1_ref[0:NZ]
    up, down = jnp.where(odd_x, got0, got1), jnp.where(odd_x, got1, got0)
    pad = jnp.zeros((6, CY), F32)

    def rows(k, at):
        pick = lambda a: jnp.sum(jnp.where(lane == at, a[:, k:k + 1], 0.0), axis=0, keepdims=True)
        return jnp.concatenate([pick(up), pick(down), pad])

    lo, hi = rows(0, 4 * sub), rows(CY - 1, (4 * sub - 1) & (CY - 1))
    first_ref[0:CX] = side0_ref[...]
    second_ref[0:CX] = side1_ref[...]
    first_ref[CX:72] = jnp.where(odd_y, lo, hi)
    second_ref[CX:72] = jnp.where(odd_y, hi, lo)


def piece(src, dst, sems, g):
    at = pl.ds(g * STEP, STEP)
    return pltpu.make_async_copy(src.at[at], dst.at[at], sems.at[g])


def lines_kernel(c_hbm, mu_hbm, mob_hbm, bx_hbm, own0_ref, own1_ref, send0_ref, send1_ref, side0_ref, side1_ref, got0_ref,
                 got1_ref, lin_hbm, rim_ref, c_ref, mu_ref, mob_ref, bx_ref, lin_ref, ch, fh, mul, mobl, mur, mobr, slo_ref,
                 shi_ref, yl_ref, yr_ref, xl_ref, xr_ref, sems):
    row, row8 = iota((CX, CY), 0), iota((8, CY), 0)
    lane = iota((CX, CY), 1)
    loads = ((c_hbm, c_ref), (mu_hbm, mu_ref), (mob_hbm, mob_ref), (bx_hbm, bx_ref))
    for g in range(NZ // STEP):
        for k, (src, dst) in enumerate(loads):
            piece(src, dst, sems.at[k], g).start()
    odd_x, odd_y = odd_at("gx"), odd_at("gy")

    def edges():
        slo_ref[...] = jnp.where(odd_y, send0_ref[...], send1_ref[...])
        shi_ref[...] = jnp.where(odd_y, send1_ref[...], send0_ref[...])
        yl_ref[...] = jnp.where(odd_y, side0_ref[...], side1_ref[...])
        yr_ref[...] = jnp.where(odd_y, side1_ref[...], side0_ref[...])
        xl_ref[...] = jnp.where(odd_x, got0_ref[...], got1_ref[...])
        xr_ref[...] = jnp.where(odd_x, got1_ref[...], got0_ref[...])
        own_lo = jnp.where(odd_x, own0_ref[0:NZ], own1_ref[0:NZ])
        own_hi = jnp.where(odd_x, own1_ref[0:NZ], own0_ref[0:NZ])
        lo, hi, left, right = slo_ref[0:CX], shi_ref[0:CX], yl_ref[0:CX], yr_ref[0:CX]

        def around(a, ref):
            up = jnp.where(row == 0, ref[CX:CX + 1], roll(a, 1, 0))
            down = jnp.where(row == CX - 1, ref[CX + 1:CX + 2], roll(a, -1, 0))
            return up + down

        c0, c1, m0 = lo, roll(lo, -1, 1), roll(lo, -2, 1)
        cm1, cm2, mm1 = roll(left, 1, 1), roll(left, 2, 1), roll(left, -1, 1)
        mu0 = potential(c0, cm1 + c1 + around(lo, slo_ref) - 4.0 * c0)
        mum1 = potential(cm1, cm2 + c0 + roll(around(left, yl_ref), 1, 1) - 4.0 * cm1)
        flux_l = (mobile(mm1, cm1) + mobile(m0, c0)) * (mu0 - mum1)
        cn, cn1, mn = hi, roll(hi, 1, 1), roll(hi, -2, 1)
        cp, cp2, mp = roll(right, -1, 1), roll(right, -2, 1), roll(right, -3, 1)
        mun = potential(cn, cn1 + cp + around(hi, shi_ref) - 4.0 * cn)
        mup = potential(cp, cn + cp2 + roll(around(right, yr_ref), -1, 1) - 4.0 * cp)
        flux_r = (mobile(mp, cp) + mobile(mn, cn)) * (mup - mun)
        first = (lane & 3) == 0
        fh[...] = jnp.where(first, flux_l, flux_r)
        ch[...] = jnp.where(first, cm1, cp)

        sub, ln = iota((NZ, CY), 0), iota((NZ, CY), 1)

        def halo_row(x_ref, own, k, mu_out, mob_out):
            a = x_ref[0:32]
            west = jnp.where(ln == ((4 * sub - 1) & (CY - 1)), yl_ref[CX + k:CX + k + 1], 0.0)
            east = jnp.where(ln == 4 * sub, yr_ref[CX + k:CX + k + 1], 0.0)
            lf = jnp.where(ln == 0, jnp.sum(west, axis=1, keepdims=True), roll(a, 1, 1))
            rt = jnp.where(ln == CY - 1, jnp.sum(east, axis=1, keepdims=True), roll(a, -1, 1))
            mu_out[...] = potential(a, x_ref[32:64] + own + lf + rt - 4.0 * a)
            mob_out[...] = mobile(x_ref[64:96], a)

        halo_row(xl_ref, own_lo, 0, mul, mobl)
        halo_row(xr_ref, own_hi, 1, mur, mobr)

    edges()

    def step(g, carry):
        for k, (src, dst) in enumerate(loads):
            piece(src, dst, sems.at[k], g).wait()
        for i in range(STEP):
            plane(g * STEP + i)
        piece(lin_ref, lin_hbm, sems.at[4], g).start()
        return carry

    def plane(z):
        at = pl.ds(z, 1)
        turn = (CY - 4 * z) & (CY - 1)
        c, mob = c_ref[z], mob_ref[z]
        hz = roll(ch[...], turn, 1)
        fz = roll(fh[...], turn, 1)
        mu = mu_ref[z] - jnp.where((lane == 0) | (lane == CY - 1), hz, 0.0)
        mu = jnp.concatenate([
            mu[0:8] - jnp.where(row8 == 0, xl_ref[at], 0.0),
            mu[8:CX - 8],
            mu[CX - 8:CX] - jnp.where(row8 == 7, xr_ref[at], 0.0),
        ])
        mu_d = jnp.where(row == CX - 1, mur[at], roll(mu, -1, 0))
        mob_d = jnp.where(row == CX - 1, mobr[at], roll(mob, -1, 0))
        fx = (mob_d + mob) * (mu_d - mu)
        f0 = (mob[0:1] + mobl[at]) * (mu[0:1] - mul[at])
        fx_up = jnp.where(row == 0, f0, roll(fx, 1, 0))
        fy = (roll(mob, -1, 1) + mob) * (roll(mu, -1, 1) - mu)
        fy = jnp.where(lane == CY - 1, fz, fy)
        fy_lf = jnp.where(lane == 0, fz, roll(fy, 1, 1))
        rhs = c + 0.01 * ((fx - fx_up) + (fy - fy_lf))
        lin = dot3(bx_ref[z], rhs, ((1,), (0,)))
        lin_ref[z] = lin
        rim_ref[z, 0:2] = lin[0:2]
        rim_ref[z, 2:4] = lin[CX - 2:CX]

    lax.fori_loop(0, NZ // STEP, step, 0)
    for g in range(NZ // STEP):
        piece(lin_ref, lin_hbm, sems.at[4], g).wait()


def reduced_kernel(r_ref, rim_ref, out_ref):
    r = r_ref[...]
    use = jnp.where((iota((4 * NZ, 4 * NZ), 0) & 3) < 2, roll(r, 2, 0), roll(r, -2, 0))
    out_ref[...] = dot3(use, rim_ref[...], ((1,), (0,)))


def wide_kernel(lin_hbm, by_hbm, rim_ref, byr_ref, lin, low, high, sems):
    ends = [
        pltpu.make_async_copy(by_hbm.at[:, pl.ds(0, 8), :], low, sems.at[NZ // STEP]),
        pltpu.make_async_copy(by_hbm.at[:, pl.ds(CY - 8, 8), :], high, sems.at[NZ // STEP + 1]),
    ]
    for copy in ends:
        copy.start()
    for g in range(NZ // STEP):
        piece(lin_hbm, lin, sems, g).start()
    for copy in ends:
        copy.wait()
    for k in range(4):
        byr_ref[pl.ds(k, NZ, stride=4), :] = high[:, 6 + k, :] if k < 2 else low[:, k - 2, :]
    lane = iota((CX, CY), 1)
    acc = jnp.zeros((CX, CY), F32)
    for g in range(NZ // STEP):
        piece(lin_hbm, lin, sems, g).wait()
        part = lin[STEP * g:STEP * (g + 1)].reshape(STEP * CX, CY)
        out = dot3(part, byr_ref[...], ((1,), (1,)))
        for i in range(STEP):
            acc = jnp.where((lane >> 2) == STEP * g + i, out[CX * i:CX * (i + 1)], acc)
    rim_ref[...] = acc


def diag_kernel(y_ref, hi_ref, lo_ref):
    n = 4 * NZ
    r, col = iota((n, 32 * NZ), 0), iota((n, 32 * NZ), 1)
    k, q = r & 3, lax.axis_index("gy")
    used = (r >> 2) * 32 + ((4 * q + k + jnp.where(k < 2, -2, 2)) & 31)
    take = jnp.where(col == used, 1.0, 0.0).astype(BF16)
    same = (iota((n, n), 0) >> 2) == (iota((n, n), 1) >> 2)
    col, ln = iota((32, n), 0), iota((32, n), 1)
    for half, ref in zip(halves(y_ref[...]), (hi_ref, lo_ref)):
        mine = jnp.dot(take, half, preferred_element_type=F32).astype(BF16)
        for p in range(8):
            pick = jnp.where(col == 4 * p + ((ln + 2) & 3), 1.0, 0.0).astype(BF16)
            full = jnp.dot(mine, pick, preferred_element_type=F32)
            ref[:, n * p:n * (p + 1)] = jnp.where(same, full, 0.0).astype(BF16)


def rims_kernel(wrim_ref, cx_ref, byr_ref, sx_ref, out_ref):
    n = 4 * NZ
    same = (iota((n, n), 0) >> 2) == (iota((n, n), 1) >> 2)
    mixed = jnp.where(same, dot3(cx_ref[...], byr_ref[...], ((1,), (1,))), 0.0)
    v = wrim_ref[...] - dot3(sx_ref[...], mixed, ((0,), (0,)))
    for q in range(8):
        out_ref[q] = v


def spread(packed, g):
    lane = iota((CX, CY), 1)
    return jnp.concatenate([jnp.where((lane >> 2) == STEP * g + i, packed, 0.0) for i in range(STEP)])


def couple_kernel(lin_hbm, by_hbm, cx_ref, sx_ref, u_hbm, lin, by, u, spikes, sems):
    for g in range(NZ // STEP):
        piece(lin_hbm, lin, sems.at[0], g).start()
        piece(by_hbm, by, sems.at[1], g).start()
    spikes[...] = jnp.transpose(sx_ref[...])

    def step(h, carry):
        for g in (2 * h, 2 * h + 1):
            fix = dot3(spread(spikes[...], g), cx_ref[...], ((1,), (0,)))
            piece(lin_hbm, lin, sems.at[0], g).wait()
            piece(by_hbm, by, sems.at[1], g).wait()
            for i in range(STEP):
                z = STEP * g + i
                vs = jnp.concatenate(halves(lin[z] - fix[CX * i:CX * (i + 1)]))
                bs = jnp.concatenate(halves(by[z]))
                all_ = lax.dot_general(vs, bs, (((1,), (1,)), ((), ())), preferred_element_type=F32)
                u[z] = all_[:CX, :CY] + (all_[:CX, CY:] + all_[CX:, :CY])
            piece(u, u_hbm, sems.at[2], g).start()
        return carry

    lax.fori_loop(0, NZ // STEP // 2, step, 0)
    for g in range(NZ // STEP):
        piece(u, u_hbm, sems.at[2], g).wait()


def last_kernel(u_hbm, g_ref, dh_ref, dl_ref, sy_ref, out_hbm, u, cy, sems):
    nt = lambda a, b: lax.dot_general(a, b, (((1,), (1,)), ((), ())), preferred_element_type=F32)
    for g in range(NZ // STEP):
        piece(u_hbm, u, sems.at[0], g).start()
    gh, gl = halves(jnp.concatenate([g_ref[q] for q in range(8)], axis=1))
    cy[...] = nt(gh, dh_ref[...]) + (nt(gh, dl_ref[...]) + nt(gl, dh_ref[...]))

    def step(g, carry):
        fix = dot3(spread(cy[...], g), sy_ref[...], ((1,), (0,)))
        piece(u_hbm, u, sems.at[0], g).wait()
        for i in range(STEP):
            z = STEP * g + i
            u[z] = u[z] - fix[CX * i:CX * (i + 1)]
        piece(u, out_hbm, sems.at[1], g).start()
        return carry

    lax.fori_loop(0, NZ // STEP, step, 0)
    for g in range(NZ // STEP):
        piece(u, out_hbm, sems.at[1], g).wait()


def shape(*dims):
    return jax.ShapeDtypeStruct(dims, F32)


def body(conc, mobility, block_x, spike_x, reduced_x, block_y, spike_y, reduced_y):
    nx, ny = lax.axis_size("gx"), lax.axis_size("gy")
    p = lax.axis_index("gx")
    hbm = lambda a: pltpu.with_memory_space_constraint(a, pltpu.HBM)
    any_space = pl.BlockSpec(memory_space=pl.ANY)
    here = pl.BlockSpec()
    full = lambda *dims: pltpu.VMEM(dims, F32)
    groups = NZ // STEP
    big, big_hbm = shape(NZ, CX, CY), pltpu.HBM((NZ, CX, CY), F32)

    def pairs(n, start):
        ends = [(i % n, (i + 1) % n) for i in range(start, start + n, 2)]
        return ends + [(b, a) for a, b in ends]

    def swap(first, second, axis, n):
        return lax.ppermute(first, axis, pairs(n, 0)), lax.ppermute(second, axis, pairs(n, 1))

    own0, own1 = pl.pallas_call(
        edge_kernel,
        in_specs=[any_space, any_space],
        out_shape=(shape(3 * NZ, CY), shape(3 * NZ, CY)),
        scratch_shapes=[full(NZ, 8, CY)] * 4 + [pltpu.SemaphoreType.DMA((4,))],
        compiler_params=CALL, name="edge",
    )(hbm(conc), hbm(mobility))
    got0, got1 = swap(own0, own1, "gx", nx)
    *side, mu, mob = pl.pallas_call(
        pack_kernel,
        in_specs=[here, here],
        out_specs=(here, here, any_space, any_space),
        out_shape=(shape(CX, CY), shape(CX, CY), big_hbm, big_hbm),
        scratch_shapes=[full(NZ, CX, CY)] * 2 + [pltpu.SemaphoreType.DMA((2, groups))],
        compiler_params=CALL, name="pack",
    )(conc, mobility)
    send0, send1 = pl.pallas_call(
        corner_kernel, out_shape=(shape(72, CY),) * 2, compiler_params=CALL, name="corner"
    )(*side, got0, got1)
    side0, side1 = swap(send0, send1, "gy", ny)

    lin, rims = pl.pallas_call(
        lines_kernel,
        in_specs=[any_space] * 4 + [here] * 8,
        out_specs=(any_space, here),
        out_shape=(big_hbm, shape(NZ, 4, CY)),
        scratch_shapes=[full(NZ, CX, CY)] * 3 + [full(NZ, CX, CX), full(NZ, CX, CY)]
        + [full(CX, CY)] * 2 + [full(NZ, CY)] * 4 + [full(72, CY)] * 4 + [full(3 * NZ, CY)] * 2
        + [pltpu.SemaphoreType.DMA((5, groups))],
        compiler_params=CALL, name="lines",
    )(hbm(conc), hbm(mu), hbm(mob), hbm(block_x), own0, own1, send0, send1, side0, side1, got0, got1)

    lin, rims, block_y, reduced_y = lax.optimization_barrier((lin, rims, block_y, reduced_y))
    sx = jnp.transpose(spike_x, (0, 2, 1)).reshape(4 * NZ, CX)
    sy = jnp.transpose(spike_y, (0, 2, 1)).reshape(4 * NZ, CY)
    wrim, byr = pl.pallas_call(
        wide_kernel,
        in_specs=[any_space] * 2,
        out_shape=(shape(CX, CY), shape(4 * NZ, CY)),
        scratch_shapes=[full(NZ, CX, CY)] + [full(NZ, 8, CY)] * 2 + [pltpu.SemaphoreType.DMA((groups + 2,))],
        compiler_params=CALL, name="wide",
    )(hbm(lin), hbm(block_y))
    dh, dl = pl.pallas_call(
        diag_kernel,
        out_shape=(jax.ShapeDtypeStruct((CY, ny * CY), BF16),) * 2,
        compiler_params=CALL, name="diag",
    )(reduced_y.reshape(NZ * 4 * ny, 4 * ny))

    mine = lax.dynamic_index_in_dim(reduced_x, p, 0, keepdims=False)
    rims = lax.all_to_all(rims, "gx", 0, 0, tiled=True)
    rims, wrim, mine = lax.optimization_barrier((rims, wrim, mine))
    solved = pl.pallas_call(
        reduced_kernel, out_shape=shape(4 * NZ, CY), compiler_params=CALL, name="reduced"
    )(mine, rims.reshape(4 * NZ, CY))
    cx = lax.all_to_all(solved.reshape(NZ, 4, CY), "gx", 0, 0, tiled=True).reshape(4 * NZ, CY)

    yrim = pl.pallas_call(rims_kernel, out_shape=shape(ny, CX, CY), compiler_params=CALL, name="rims")(
        wrim, cx, byr, sx
    )
    yall = lax.all_to_all(yrim, "gy", 0, 0, tiled=True)
    u = pl.pallas_call(
        couple_kernel,
        in_specs=[any_space, any_space, here, here],
        out_specs=any_space,
        out_shape=big_hbm,
        scratch_shapes=[full(NZ, CX, CY), full(NZ, CY, CY), full(NZ, CX, CY), full(CX, CY),
                        pltpu.SemaphoreType.DMA((3, groups))],
        compiler_params=CALL, name="couple",
    )(hbm(lin), hbm(block_y), cx, sx)
    return pl.pallas_call(
        last_kernel,
        in_specs=[any_space] + [here] * 4,
        out_specs=any_space,
        out_shape=big_hbm,
        scratch_shapes=[full(NZ, CX, CY), full(CX, CY), pltpu.SemaphoreType.DMA((2, groups))],
        compiler_params=CALL, name="last",
    )(hbm(u), yall, dh, dl, sy)


def solution(mesh):
    in_specs = (
        P(None, "gx", "gy"),
        P(None, "gx", "gy"),
        P(None, "gx", None),
        P(None, "gx", None),
        P(),
        P(None, "gy", None),
        P(None, "gy", None),
        P(),
    )
    out_specs = P(None, "gx", "gy")
    return jax.shard_map(body, mesh=mesh, in_specs=in_specs, out_specs=out_specs, check_vma=False)
```

```python
import jax
import jax.numpy as jnp
from jax import lax
from jax.experimental import pallas as pl
from jax.experimental.pallas import tpu as pltpu
from jax.sharding import PartitionSpec as P

NZ, CX, CY = 32, 64, 128
STEP, HALF = 8, 4
F32, BF16 = jnp.float32, jnp.bfloat16
CALL = pltpu.CompilerParams(vmem_limit_bytes=12 * 1024 * 1024)


def halves(a):
    hi = a.astype(BF16)
    return hi, (a - hi.astype(F32)).astype(BF16)


def dot3(a, b, dims):
    ah, al = halves(a)
    bh, bl = halves(b)
    one = lambda x, y: lax.dot_general(x, y, (dims, ((), ())), preferred_element_type=F32)
    return one(ah, bh) + (one(ah, bl) + one(al, bh))


def iota(shape, axis):
    return lax.broadcasted_iota(jnp.int32, shape, axis)


def roll(a, shift, axis):
    if isinstance(shift, int) and shift % a.shape[axis] == 0:
        return a
    if isinstance(shift, int):
        shift = shift % a.shape[axis]
    return pltpu.roll(a, shift, axis)


def potential(c, lap):
    return c * c * c - c - lap


def mobile(prefactor, c):
    sq = c * c
    return prefactor * (0.25 + sq) / (1.0 + sq)


def odd_at(axis):
    return (lax.axis_index(axis) & 1) == 1


def edge_kernel(c_ref, m_ref, first_ref, second_ref, ct, cb, mt, mb, sems):
    top, bottom = pl.ds(0, 8), pl.ds(CX - 8, 8)
    copies = [
        pltpu.make_async_copy(c_ref.at[:, top, :], ct, sems.at[0]),
        pltpu.make_async_copy(m_ref.at[:, top, :], mt, sems.at[1]),
        pltpu.make_async_copy(c_ref.at[:, bottom, :], cb, sems.at[2]),
        pltpu.make_async_copy(m_ref.at[:, bottom, :], mb, sems.at[3]),
    ]
    for copy in copies:
        copy.start()
    for copy in copies:
        copy.wait()
    odd = odd_at("gx")
    rows = ((ct[:, 0, :], cb[:, 7, :]), (ct[:, 1, :], cb[:, 6, :]), (mt[:, 0, :], mb[:, 7, :]))
    for k, (lo, hi) in enumerate(rows):
        first_ref[NZ * k:NZ * (k + 1)] = jnp.where(odd, lo, hi)
        second_ref[NZ * k:NZ * (k + 1)] = jnp.where(odd, hi, lo)


def pack_kernel(c_ref, m_ref, first_ref, second_ref, mu_ref, mobx_ref, moby_ref):
    row, lane = iota((CX, CY), 0), iota((CX, CY), 1)
    lo = jnp.zeros((CX, CY), F32)
    hi = jnp.zeros((CX, CY), F32)
    for z in range(NZ):
        c = roll(c_ref[z], 4 * z, 1)
        m = roll(m_ref[z], 4 * z + 2, 1)
        a, b = (4 * z - 2) % CY, 4 * z
        lo = jnp.where((lane >= b) & (lane <= b + 1), c, lo)
        lo = jnp.where(lane == b + 2, m, lo)
        hi = jnp.where((lane >= a) & (lane <= a + 1), c, hi)
        hi = jnp.where(lane == b + 1, m, hi)
    odd = odd_at("gy")
    first_ref[...] = jnp.where(odd, lo, hi)
    second_ref[...] = jnp.where(odd, hi, lo)

    def step(g, carry):
        for i in range(STEP):
            z = g * STEP + i
            c = c_ref[z]
            up = jnp.where(row == 0, 0.0, roll(c, 1, 0))
            down = jnp.where(row == CX - 1, 0.0, roll(c, -1, 0))
            lf = jnp.where(lane == 0, 0.0, roll(c, 1, 1))
            rt = jnp.where(lane == CY - 1, 0.0, roll(c, -1, 1))
            mu_ref[z] = potential(c, up + down + lf + rt - 4.0 * c)
            mob = mobile(m_ref[z], c)
            mobx_ref[z] = mob + roll(mob, -1, 0)
            moby_ref[z] = mob + roll(mob, -1, 1)
        return carry

    lax.fori_loop(0, NZ // STEP, step, 0)


def corner_kernel(side0_ref, side1_ref, got0_ref, got1_ref, first_ref, second_ref):
    sub, lane = iota((NZ, CY), 0), iota((NZ, CY), 1)
    odd_x, odd_y = odd_at("gx"), odd_at("gy")
    got0, got1 = got0_ref[0:NZ], got1_ref[0:NZ]
    up, down = jnp.where(odd_x, got0, got1), jnp.where(odd_x, got1, got0)
    pad = jnp.zeros((6, CY), F32)

    def rows(k, at):
        pick = lambda a: jnp.sum(jnp.where(lane == at, a[:, k:k + 1], 0.0), axis=0, keepdims=True)
        return jnp.concatenate([pick(up), pick(down), pad])

    lo, hi = rows(0, 4 * sub), rows(CY - 1, (4 * sub - 1) & (CY - 1))
    first_ref[0:CX] = side0_ref[...]
    second_ref[0:CX] = side1_ref[...]
    first_ref[CX:72] = jnp.where(odd_y, lo, hi)
    second_ref[CX:72] = jnp.where(odd_y, hi, lo)


def piece(src, dst, sems, g, size=STEP):
    at = pl.ds(g * size, size)
    return pltpu.make_async_copy(src.at[at], dst.at[at], sems.at[g])


def lines_kernel(c_ref, mu_ref, mobx_ref, moby_ref, bx_ref, own0_ref, own1_ref, send0_ref, send1_ref, side0_ref, side1_ref, got0_ref,
                 got1_ref, lin_hbm, rim_ref, lin_ref, ch, fh, mul, mobl, mur, mobr, slo_ref,
                 shi_ref, yl_ref, yr_ref, xl_ref, xr_ref, sems):
    row, row8 = iota((CX, CY), 0), iota((8, CY), 0)
    lane = iota((CX, CY), 1)
    odd_x, odd_y = odd_at("gx"), odd_at("gy")

    def edges():
        slo_ref[...] = jnp.where(odd_y, send0_ref[...], send1_ref[...])
        shi_ref[...] = jnp.where(odd_y, send1_ref[...], send0_ref[...])
        yl_ref[...] = jnp.where(odd_y, side0_ref[...], side1_ref[...])
        yr_ref[...] = jnp.where(odd_y, side1_ref[...], side0_ref[...])
        xl_ref[...] = jnp.where(odd_x, got0_ref[...], got1_ref[...])
        xr_ref[...] = jnp.where(odd_x, got1_ref[...], got0_ref[...])
        own_lo = jnp.where(odd_x, own0_ref[...], own1_ref[...])
        own_hi = jnp.where(odd_x, own1_ref[...], own0_ref[...])
        lo, hi, left, right = slo_ref[0:CX], shi_ref[0:CX], yl_ref[0:CX], yr_ref[0:CX]

        def around(a, ref):
            up = jnp.where(row == 0, ref[CX:CX + 1], roll(a, 1, 0))
            down = jnp.where(row == CX - 1, ref[CX + 1:CX + 2], roll(a, -1, 0))
            return up + down

        c0, c1, m0 = lo, roll(lo, -1, 1), roll(lo, -2, 1)
        cm1, cm2, mm1 = roll(left, 1, 1), roll(left, 2, 1), roll(left, -1, 1)
        mu0 = potential(c0, cm1 + c1 + around(lo, slo_ref) - 4.0 * c0)
        mum1 = potential(cm1, cm2 + c0 + roll(around(left, yl_ref), 1, 1) - 4.0 * cm1)
        flux_l = (mobile(mm1, cm1) + mobile(m0, c0)) * (mu0 - mum1)
        cn, cn1, mn = hi, roll(hi, 1, 1), roll(hi, -2, 1)
        cp, cp2, mp = roll(right, -1, 1), roll(right, -2, 1), roll(right, -3, 1)
        mun = potential(cn, cn1 + cp + around(hi, shi_ref) - 4.0 * cn)
        mup = potential(cp, cn + cp2 + roll(around(right, yr_ref), -1, 1) - 4.0 * cp)
        flux_r = (mobile(mp, cp) + mobile(mn, cn)) * (mup - mun)
        first = (lane & 3) == 0
        fh[...] = jnp.where(first, flux_l, flux_r)
        ch[...] = jnp.where(first, cm1, cp)

        sub, ln = iota((NZ, CY), 0), iota((NZ, CY), 1)

        def halo_row(x_ref, own, k, mu_out, mob_out):
            a = x_ref[0:32]
            west = jnp.where(ln == ((4 * sub - 1) & (CY - 1)), yl_ref[CX + k:CX + k + 1], 0.0)
            east = jnp.where(ln == 4 * sub, yr_ref[CX + k:CX + k + 1], 0.0)
            lf = jnp.where(ln == 0, jnp.sum(west, axis=1, keepdims=True), roll(a, 1, 1))
            rt = jnp.where(ln == CY - 1, jnp.sum(east, axis=1, keepdims=True), roll(a, -1, 1))
            mu_out[...] = potential(a, x_ref[32:64] + own[0:32] + lf + rt - 4.0 * a)
            mob_out[...] = mobile(x_ref[64:96], a) + mobile(own[64:96], own[0:32])

        halo_row(xl_ref, own_lo, 0, mul, mobl)
        halo_row(xr_ref, own_hi, 1, mur, mobr)

    edges()

    def step(g, carry):
        for i in range(STEP):
            plane(g * STEP + i)
            if i % HALF == HALF - 1:
                piece(lin_ref, lin_hbm, sems, 2 * g + i // HALF, HALF).start()
        return carry

    def plane(z):
        at = pl.ds(z, 1)
        turn = (CY - 4 * z) & (CY - 1)
        c, mobx = c_ref[z], mobx_ref[z]
        hz = roll(ch[...], turn, 1)
        fz = roll(fh[...], turn, 1)
        mu = mu_ref[z] - jnp.where((lane == 0) | (lane == CY - 1), hz, 0.0)
        mu = jnp.concatenate([
            mu[0:8] - jnp.where(row8 == 0, xl_ref[at], 0.0),
            mu[8:CX - 8],
            mu[CX - 8:CX] - jnp.where(row8 == 7, xr_ref[at], 0.0),
        ])
        mu_d = jnp.where(row == CX - 1, mur[at], roll(mu, -1, 0))
        mobx = jnp.concatenate([mobx[:CX - 8], jnp.where(row8 == 7, mobr[at], mobx[CX - 8:])])
        fx = mobx * (mu_d - mu)
        f0 = mobl[at] * (mu[0:1] - mul[at])
        fx_up = jnp.where(row == 0, f0, roll(fx, 1, 0))
        fy = moby_ref[z] * (roll(mu, -1, 1) - mu)
        fy = jnp.where(lane == CY - 1, fz, fy)
        fy_lf = jnp.where(lane == 0, fz, roll(fy, 1, 1))
        rhs = c + 0.01 * ((fx - fx_up) + (fy - fy_lf))
        lin = dot3(bx_ref[z], rhs, ((1,), (0,)))
        lin_ref[z] = lin
        rim_ref[z, 0:2] = lin[0:2]
        rim_ref[z, 2:4] = lin[CX - 2:CX]

    lax.fori_loop(0, NZ // STEP, step, 0)
    for g in range(NZ // HALF):
        piece(lin_ref, lin_hbm, sems, g, HALF).wait()


def reduced_kernel(r_ref, rim_ref, out_ref):
    r = r_ref[...]
    use = jnp.where((iota((4 * NZ, 4 * NZ), 0) & 3) < 2, roll(r, 2, 0), roll(r, -2, 0))
    out_ref[...] = dot3(use, rim_ref[...], ((1,), (0,)))


def wide_kernel(lin_hbm, by_hbm, rim_ref, byr_ref, lin, low, high, sems):
    ends = [
        pltpu.make_async_copy(by_hbm.at[:, pl.ds(0, 8), :], low, sems.at[NZ // STEP]),
        pltpu.make_async_copy(by_hbm.at[:, pl.ds(CY - 8, 8), :], high, sems.at[NZ // STEP + 1]),
    ]
    for copy in ends:
        copy.start()
    for g in range(NZ // STEP):
        piece(lin_hbm, lin, sems, g).start()
    for copy in ends:
        copy.wait()
    for k in range(4):
        byr_ref[pl.ds(k, NZ, stride=4), :] = high[:, 6 + k, :] if k < 2 else low[:, k - 2, :]
    lane = iota((CX, CY), 1)
    acc = jnp.zeros((CX, CY), F32)
    for g in range(NZ // STEP):
        piece(lin_hbm, lin, sems, g).wait()
        part = lin[STEP * g:STEP * (g + 1)].reshape(STEP * CX, CY)
        out = dot3(part, byr_ref[...], ((1,), (1,)))
        for i in range(STEP):
            acc = jnp.where((lane >> 2) == STEP * g + i, out[CX * i:CX * (i + 1)], acc)
    rim_ref[...] = acc


def diag_kernel(y_ref, hi_ref, lo_ref):
    n = 4 * NZ
    r, col = iota((n, 32 * NZ), 0), iota((n, 32 * NZ), 1)
    k, q = r & 3, lax.axis_index("gy")
    used = (r >> 2) * 32 + ((4 * q + k + jnp.where(k < 2, -2, 2)) & 31)
    take = jnp.where(col == used, 1.0, 0.0).astype(BF16)
    same = (iota((n, n), 0) >> 2) == (iota((n, n), 1) >> 2)
    col, ln = iota((32, n), 0), iota((32, n), 1)
    for half, ref in zip(halves(y_ref[...]), (hi_ref, lo_ref)):
        mine = jnp.dot(take, half, preferred_element_type=F32).astype(BF16)
        for p in range(8):
            pick = jnp.where(col == 4 * p + ((ln + 2) & 3), 1.0, 0.0).astype(BF16)
            full = jnp.dot(mine, pick, preferred_element_type=F32)
            ref[:, n * p:n * (p + 1)] = jnp.where(same, full, 0.0).astype(BF16)


def rims_kernel(wrim_ref, cx_ref, byr_ref, sx_ref, out_ref):
    n = 4 * NZ
    same = (iota((n, n), 0) >> 2) == (iota((n, n), 1) >> 2)
    mixed = jnp.where(same, dot3(cx_ref[...], byr_ref[...], ((1,), (1,))), 0.0)
    v = wrim_ref[...] - dot3(sx_ref[...], mixed, ((0,), (0,)))
    for q in range(8):
        out_ref[q] = v


def spread(packed, g):
    lane = iota((CX, CY), 1)
    return jnp.concatenate([jnp.where((lane >> 2) == STEP * g + i, packed, 0.0) for i in range(STEP)])


def couple_kernel(lin_hbm, by_hbm, cx_ref, sx_ref, u_hbm, lin, by, u, spikes, sems):
    for g in range(NZ // STEP):
        piece(lin_hbm, lin, sems.at[0], g).start()
        piece(by_hbm, by, sems.at[1], g).start()
    spikes[...] = jnp.transpose(sx_ref[...])

    def step(h, carry):
        for g in (2 * h, 2 * h + 1):
            fix = dot3(spread(spikes[...], g), cx_ref[...], ((1,), (0,)))
            piece(lin_hbm, lin, sems.at[0], g).wait()
            piece(by_hbm, by, sems.at[1], g).wait()
            for i in range(STEP):
                z = STEP * g + i
                vs = jnp.concatenate(halves(lin[z] - fix[CX * i:CX * (i + 1)]))
                bs = jnp.concatenate(halves(by[z]))
                all_ = lax.dot_general(vs, bs, (((1,), (1,)), ((), ())), preferred_element_type=F32)
                u[z] = all_[:CX, :CY] + (all_[:CX, CY:] + all_[CX:, :CY])
            piece(u, u_hbm, sems.at[2], g).start()
        return carry

    lax.fori_loop(0, NZ // STEP // 2, step, 0)
    for g in range(NZ // STEP):
        piece(u, u_hbm, sems.at[2], g).wait()


def last_kernel(u_hbm, g_ref, dh_ref, dl_ref, sy_ref, out_hbm, u, cy, sems):
    nt = lambda a, b: lax.dot_general(a, b, (((1,), (1,)), ((), ())), preferred_element_type=F32)
    for g in range(NZ // STEP):
        piece(u_hbm, u, sems.at[0], g).start()
    gh, gl = halves(jnp.concatenate([g_ref[q] for q in range(8)], axis=1))
    cy[...] = nt(gh, dh_ref[...]) + (nt(gh, dl_ref[...]) + nt(gl, dh_ref[...]))

    def step(g, carry):
        fix = dot3(spread(cy[...], g), sy_ref[...], ((1,), (0,)))
        piece(u_hbm, u, sems.at[0], g).wait()
        for i in range(STEP):
            z = STEP * g + i
            u[z] = u[z] - fix[CX * i:CX * (i + 1)]
        piece(u, out_hbm, sems.at[1], g).start()
        return carry

    lax.fori_loop(0, NZ // STEP, step, 0)
    for g in range(NZ // STEP):
        piece(u, out_hbm, sems.at[1], g).wait()


def shape(*dims):
    return jax.ShapeDtypeStruct(dims, F32)


def body(conc, mobility, block_x, spike_x, reduced_x, block_y, spike_y, reduced_y):
    nx, ny = lax.axis_size("gx"), lax.axis_size("gy")
    p = lax.axis_index("gx")
    hbm = lambda a: pltpu.with_memory_space_constraint(a, pltpu.HBM)
    any_space = pl.BlockSpec(memory_space=pl.ANY)
    here = pl.BlockSpec()
    full = lambda *dims: pltpu.VMEM(dims, F32)
    groups = NZ // STEP
    big, big_hbm = shape(NZ, CX, CY), pltpu.HBM((NZ, CX, CY), F32)

    def pairs(n, start):
        ends = [(i % n, (i + 1) % n) for i in range(start, start + n, 2)]
        return ends + [(b, a) for a, b in ends]

    def swap(first, second, axis, n):
        return lax.ppermute(first, axis, pairs(n, 0)), lax.ppermute(second, axis, pairs(n, 1))

    own0, own1 = pl.pallas_call(
        edge_kernel,
        in_specs=[any_space, any_space],
        out_shape=(shape(3 * NZ, CY), shape(3 * NZ, CY)),
        scratch_shapes=[full(NZ, 8, CY)] * 4 + [pltpu.SemaphoreType.DMA((4,))],
        compiler_params=CALL, name="edge",
    )(hbm(conc), hbm(mobility))
    got0, got1 = swap(own0, own1, "gx", nx)
    *side, mu, mobx, moby = pl.pallas_call(
        pack_kernel,
        out_shape=(shape(CX, CY),) * 2 + (shape(NZ, CX, CY),) * 3,
        compiler_params=CALL, name="pack",
    )(conc, mobility)
    send0, send1 = pl.pallas_call(
        corner_kernel, out_shape=(shape(72, CY),) * 2, compiler_params=CALL, name="corner"
    )(*side, got0, got1)
    side0, side1 = swap(send0, send1, "gy", ny)

    lin, rims = pl.pallas_call(
        lines_kernel,
                out_specs=(any_space, here),
        out_shape=(big_hbm, shape(NZ, 4, CY)),
        scratch_shapes=[full(NZ, CX, CY)]
        + [full(CX, CY)] * 2 + [full(NZ, CY)] * 4 + [full(72, CY)] * 4 + [full(3 * NZ, CY)] * 2
        + [pltpu.SemaphoreType.DMA((2 * groups,))],
        compiler_params=CALL, name="lines",
    )(conc, mu, mobx, moby, block_x, own0, own1, send0, send1, side0, side1, got0, got1)

    lin, rims, block_y, reduced_y = lax.optimization_barrier((lin, rims, block_y, reduced_y))
    sx = jnp.transpose(spike_x, (0, 2, 1)).reshape(4 * NZ, CX)
    sy = jnp.transpose(spike_y, (0, 2, 1)).reshape(4 * NZ, CY)
    wrim, byr = pl.pallas_call(
        wide_kernel,
        in_specs=[any_space] * 2,
        out_shape=(shape(CX, CY), shape(4 * NZ, CY)),
        scratch_shapes=[full(NZ, CX, CY)] + [full(NZ, 8, CY)] * 2 + [pltpu.SemaphoreType.DMA((groups + 2,))],
        compiler_params=CALL, name="wide",
    )(hbm(lin), hbm(block_y))
    dh, dl = pl.pallas_call(
        diag_kernel,
        out_shape=(jax.ShapeDtypeStruct((CY, ny * CY), BF16),) * 2,
        compiler_params=CALL, name="diag",
    )(reduced_y.reshape(NZ * 4 * ny, 4 * ny))

    mine = lax.dynamic_index_in_dim(reduced_x, p, 0, keepdims=False)
    rims = lax.all_to_all(rims, "gx", 0, 0, tiled=True)
    rims, wrim, mine = lax.optimization_barrier((rims, wrim, mine))
    solved = pl.pallas_call(
        reduced_kernel, out_shape=shape(4 * NZ, CY), compiler_params=CALL, name="reduced"
    )(mine, rims.reshape(4 * NZ, CY))
    cx = lax.all_to_all(solved.reshape(NZ, 4, CY), "gx", 0, 0, tiled=True).reshape(4 * NZ, CY)

    yrim = pl.pallas_call(rims_kernel, out_shape=shape(ny, CX, CY), compiler_params=CALL, name="rims")(
        wrim, cx, byr, sx
    )
    yall = lax.all_to_all(yrim, "gy", 0, 0, tiled=True)
    u = pl.pallas_call(
        couple_kernel,
        in_specs=[any_space, any_space, here, here],
        out_specs=any_space,
        out_shape=big_hbm,
        scratch_shapes=[full(NZ, CX, CY), full(NZ, CY, CY), full(NZ, CX, CY), full(CX, CY),
                        pltpu.SemaphoreType.DMA((3, groups))],
        compiler_params=CALL, name="couple",
    )(hbm(lin), hbm(block_y), cx, sx)
    return pl.pallas_call(
        last_kernel,
        in_specs=[any_space] + [here] * 4,
        out_specs=any_space,
        out_shape=big_hbm,
        scratch_shapes=[full(NZ, CX, CY), full(CX, CY), pltpu.SemaphoreType.DMA((2, groups))],
        compiler_params=CALL, name="last",
    )(hbm(u), yall, dh, dl, sy)


def solution(mesh):
    in_specs = (
        P(None, "gx", "gy"),
        P(None, "gx", "gy"),
        P(None, "gx", None),
        P(None, "gx", None),
        P(),
        P(None, "gy", None),
        P(None, "gy", None),
        P(),
    )
    out_specs = P(None, "gx", "gy")
    return jax.shard_map(body, mesh=mesh, in_specs=in_specs, out_specs=out_specs, check_vma=False)
```

```python
import jax
import jax.numpy as jnp
from jax import lax
from jax.experimental import pallas as pl
from jax.experimental.pallas import tpu as pltpu
from jax.sharding import PartitionSpec as P

NZ, CX, CY = 32, 64, 128
STEP, HALF = 8, 4
F32, BF16 = jnp.float32, jnp.bfloat16
CALL = pltpu.CompilerParams(vmem_limit_bytes=12 * 1024 * 1024)


def halves(a):
    hi = a.astype(BF16)
    return hi, (a - hi.astype(F32)).astype(BF16)


def dot3(a, b, dims):
    ah, al = halves(a)
    bh, bl = halves(b)
    one = lambda x, y: lax.dot_general(x, y, (dims, ((), ())), preferred_element_type=F32)
    return one(ah, bh) + (one(ah, bl) + one(al, bh))


def iota(shape, axis):
    return lax.broadcasted_iota(jnp.int32, shape, axis)


def roll(a, shift, axis):
    if isinstance(shift, int) and shift % a.shape[axis] == 0:
        return a
    if isinstance(shift, int):
        shift = shift % a.shape[axis]
    return pltpu.roll(a, shift, axis)


def potential(c, lap):
    return c * c * c - c - lap


def mobile(prefactor, c):
    sq = c * c
    return prefactor * (0.25 + sq) / (1.0 + sq)


def odd_at(axis):
    return (lax.axis_index(axis) & 1) == 1


def edge_kernel(c_ref, m_ref, first_ref, second_ref, ct, cb, mt, mb, sems):
    top, bottom = pl.ds(0, 8), pl.ds(CX - 8, 8)
    copies = [
        pltpu.make_async_copy(c_ref.at[:, top, :], ct, sems.at[0]),
        pltpu.make_async_copy(m_ref.at[:, top, :], mt, sems.at[1]),
        pltpu.make_async_copy(c_ref.at[:, bottom, :], cb, sems.at[2]),
        pltpu.make_async_copy(m_ref.at[:, bottom, :], mb, sems.at[3]),
    ]
    for copy in copies:
        copy.start()
    for copy in copies:
        copy.wait()
    odd = odd_at("gx")
    rows = ((ct[:, 0, :], cb[:, 7, :]), (ct[:, 1, :], cb[:, 6, :]), (mt[:, 0, :], mb[:, 7, :]))
    for k, (lo, hi) in enumerate(rows):
        first_ref[NZ * k:NZ * (k + 1)] = jnp.where(odd, lo, hi)
        second_ref[NZ * k:NZ * (k + 1)] = jnp.where(odd, hi, lo)


def pack_kernel(c_ref, m_ref, first_ref, second_ref, mu_ref, mobx_ref, moby_ref):
    row, lane = iota((CX, CY), 0), iota((CX, CY), 1)
    lo = jnp.zeros((CX, CY), F32)
    hi = jnp.zeros((CX, CY), F32)
    for z in range(NZ):
        c = roll(c_ref[z], 4 * z, 1)
        m = roll(m_ref[z], 4 * z + 2, 1)
        a, b = (4 * z - 2) % CY, 4 * z
        lo = jnp.where((lane >= b) & (lane <= b + 1), c, lo)
        lo = jnp.where(lane == b + 2, m, lo)
        hi = jnp.where((lane >= a) & (lane <= a + 1), c, hi)
        hi = jnp.where(lane == b + 1, m, hi)
    odd = odd_at("gy")
    first_ref[...] = jnp.where(odd, lo, hi)
    second_ref[...] = jnp.where(odd, hi, lo)

    def step(g, carry):
        for i in range(STEP):
            z = g * STEP + i
            c = c_ref[z]
            up = jnp.where(row == 0, 0.0, roll(c, 1, 0))
            down = jnp.where(row == CX - 1, 0.0, roll(c, -1, 0))
            lf = jnp.where(lane == 0, 0.0, roll(c, 1, 1))
            rt = jnp.where(lane == CY - 1, 0.0, roll(c, -1, 1))
            mu_ref[z] = potential(c, up + down + lf + rt - 4.0 * c)
            mob = mobile(m_ref[z], c)
            mobx_ref[z] = mob + roll(mob, -1, 0)
            moby_ref[z] = mob + roll(mob, -1, 1)
        return carry

    lax.fori_loop(0, NZ // STEP, step, 0)


def corner_kernel(side0_ref, side1_ref, got0_ref, got1_ref, first_ref, second_ref):
    sub, lane = iota((NZ, CY), 0), iota((NZ, CY), 1)
    odd_x, odd_y = odd_at("gx"), odd_at("gy")
    got0, got1 = got0_ref[0:NZ], got1_ref[0:NZ]
    up, down = jnp.where(odd_x, got0, got1), jnp.where(odd_x, got1, got0)
    pad = jnp.zeros((6, CY), F32)

    def rows(k, at):
        pick = lambda a: jnp.sum(jnp.where(lane == at, a[:, k:k + 1], 0.0), axis=0, keepdims=True)
        return jnp.concatenate([pick(up), pick(down), pad])

    lo, hi = rows(0, 4 * sub), rows(CY - 1, (4 * sub - 1) & (CY - 1))
    first_ref[0:CX] = side0_ref[...]
    second_ref[0:CX] = side1_ref[...]
    first_ref[CX:72] = jnp.where(odd_y, lo, hi)
    second_ref[CX:72] = jnp.where(odd_y, hi, lo)


def piece(src, dst, sems, g, size=STEP):
    at = pl.ds(g * size, size)
    return pltpu.make_async_copy(src.at[at], dst.at[at], sems.at[g])


def lines_kernel(c_ref, mu_ref, mobx_ref, moby_ref, bx_ref, own0_ref, own1_ref, send0_ref, send1_ref, side0_ref, side1_ref, got0_ref,
                 got1_ref, lin_hbm, rim_hbm, lin_ref, rim_ref, ch, fh, mul, mobl, mur, mobr, slo_ref,
                 shi_ref, yl_ref, yr_ref, xl_ref, xr_ref, sems):
    row, row8 = iota((CX, CY), 0), iota((8, CY), 0)
    lane = iota((CX, CY), 1)
    odd_x, odd_y = odd_at("gx"), odd_at("gy")

    def edges():
        slo_ref[...] = jnp.where(odd_y, send0_ref[...], send1_ref[...])
        shi_ref[...] = jnp.where(odd_y, send1_ref[...], send0_ref[...])
        yl_ref[...] = jnp.where(odd_y, side0_ref[...], side1_ref[...])
        yr_ref[...] = jnp.where(odd_y, side1_ref[...], side0_ref[...])
        xl_ref[...] = jnp.where(odd_x, got0_ref[...], got1_ref[...])
        xr_ref[...] = jnp.where(odd_x, got1_ref[...], got0_ref[...])
        own_lo = jnp.where(odd_x, own0_ref[...], own1_ref[...])
        own_hi = jnp.where(odd_x, own1_ref[...], own0_ref[...])
        lo, hi, left, right = slo_ref[0:CX], shi_ref[0:CX], yl_ref[0:CX], yr_ref[0:CX]

        def around(a, ref):
            up = jnp.where(row == 0, ref[CX:CX + 1], roll(a, 1, 0))
            down = jnp.where(row == CX - 1, ref[CX + 1:CX + 2], roll(a, -1, 0))
            return up + down

        c0, c1, m0 = lo, roll(lo, -1, 1), roll(lo, -2, 1)
        cm1, cm2, mm1 = roll(left, 1, 1), roll(left, 2, 1), roll(left, -1, 1)
        mu0 = potential(c0, cm1 + c1 + around(lo, slo_ref) - 4.0 * c0)
        mum1 = potential(cm1, cm2 + c0 + roll(around(left, yl_ref), 1, 1) - 4.0 * cm1)
        flux_l = (mobile(mm1, cm1) + mobile(m0, c0)) * (mu0 - mum1)
        cn, cn1, mn = hi, roll(hi, 1, 1), roll(hi, -2, 1)
        cp, cp2, mp = roll(right, -1, 1), roll(right, -2, 1), roll(right, -3, 1)
        mun = potential(cn, cn1 + cp + around(hi, shi_ref) - 4.0 * cn)
        mup = potential(cp, cn + cp2 + roll(around(right, yr_ref), -1, 1) - 4.0 * cp)
        flux_r = (mobile(mp, cp) + mobile(mn, cn)) * (mup - mun)
        first = (lane & 3) == 0
        fh[...] = jnp.where(first, flux_l, flux_r)
        ch[...] = jnp.where(first, cm1, cp)

        sub, ln = iota((NZ, CY), 0), iota((NZ, CY), 1)

        def halo_row(x_ref, own, k, mu_out, mob_out):
            a = x_ref[0:32]
            west = jnp.where(ln == ((4 * sub - 1) & (CY - 1)), yl_ref[CX + k:CX + k + 1], 0.0)
            east = jnp.where(ln == 4 * sub, yr_ref[CX + k:CX + k + 1], 0.0)
            lf = jnp.where(ln == 0, jnp.sum(west, axis=1, keepdims=True), roll(a, 1, 1))
            rt = jnp.where(ln == CY - 1, jnp.sum(east, axis=1, keepdims=True), roll(a, -1, 1))
            mu_out[...] = potential(a, x_ref[32:64] + own[0:32] + lf + rt - 4.0 * a)
            mob_out[...] = mobile(x_ref[64:96], a) + mobile(own[64:96], own[0:32])

        halo_row(xl_ref, own_lo, 0, mul, mobl)
        halo_row(xr_ref, own_hi, 1, mur, mobr)

    edges()

    def step(g, carry):
        for i in range(STEP):
            plane(g * STEP + i)
            if i % HALF == HALF - 1:
                piece(lin_ref, lin_hbm, sems.at[0], 2 * g + i // HALF, HALF).start()
                piece(rim_ref, rim_hbm, sems.at[1], 2 * g + i // HALF, HALF).start()
        return carry

    def plane(z):
        at = pl.ds(z, 1)
        turn = (CY - 4 * z) & (CY - 1)
        c, mobx = c_ref[z], mobx_ref[z]
        hz = roll(ch[...], turn, 1)
        fz = roll(fh[...], turn, 1)
        mu = mu_ref[z] - jnp.where((lane == 0) | (lane == CY - 1), hz, 0.0)
        mu = jnp.concatenate([
            mu[0:8] - jnp.where(row8 == 0, xl_ref[at], 0.0),
            mu[8:CX - 8],
            mu[CX - 8:CX] - jnp.where(row8 == 7, xr_ref[at], 0.0),
        ])
        mu_d = jnp.where(row == CX - 1, mur[at], roll(mu, -1, 0))
        mobx = jnp.concatenate([mobx[:CX - 8], jnp.where(row8 == 7, mobr[at], mobx[CX - 8:])])
        fx = mobx * (mu_d - mu)
        f0 = mobl[at] * (mu[0:1] - mul[at])
        fx_up = jnp.where(row == 0, f0, roll(fx, 1, 0))
        fy = moby_ref[z] * (roll(mu, -1, 1) - mu)
        fy = jnp.where(lane == CY - 1, fz, fy)
        fy_lf = jnp.where(lane == 0, fz, roll(fy, 1, 1))
        rhs = c + 0.01 * ((fx - fx_up) + (fy - fy_lf))
        lin = dot3(bx_ref[z], rhs, ((1,), (0,)))
        lin_ref[z] = lin
        rim_ref[z, 0:2] = lin[0:2]
        rim_ref[z, 2:4] = lin[CX - 2:CX]

    lax.fori_loop(0, NZ // STEP, step, 0)
    for g in range(NZ // HALF):
        piece(lin_ref, lin_hbm, sems.at[0], g, HALF).wait()
        piece(rim_ref, rim_hbm, sems.at[1], g, HALF).wait()


def reduced_kernel(r_ref, rim_ref, out_ref):
    r = r_ref[...]
    use = jnp.where((iota((4 * NZ, 4 * NZ), 0) & 3) < 2, roll(r, 2, 0), roll(r, -2, 0))
    out_ref[...] = dot3(use, rim_ref[...], ((1,), (0,)))


def wide_kernel(lin_hbm, by_hbm, rim_ref, byr_ref, lin, low, high, sems):
    ends = [
        pltpu.make_async_copy(by_hbm.at[:, pl.ds(0, 8), :], low, sems.at[NZ // STEP]),
        pltpu.make_async_copy(by_hbm.at[:, pl.ds(CY - 8, 8), :], high, sems.at[NZ // STEP + 1]),
    ]
    for copy in ends:
        copy.start()
    for g in range(NZ // STEP):
        piece(lin_hbm, lin, sems, g).start()
    for copy in ends:
        copy.wait()
    for k in range(4):
        byr_ref[pl.ds(k, NZ, stride=4), :] = high[:, 6 + k, :] if k < 2 else low[:, k - 2, :]
    lane = iota((CX, CY), 1)
    acc = jnp.zeros((CX, CY), F32)
    for g in range(NZ // STEP):
        piece(lin_hbm, lin, sems, g).wait()
        part = lin[STEP * g:STEP * (g + 1)].reshape(STEP * CX, CY)
        out = dot3(part, byr_ref[...], ((1,), (1,)))
        for i in range(STEP):
            acc = jnp.where((lane >> 2) == STEP * g + i, out[CX * i:CX * (i + 1)], acc)
    rim_ref[...] = acc


def diag_kernel(y_ref, hi_ref, lo_ref):
    n = 4 * NZ
    r, col = iota((n, 32 * NZ), 0), iota((n, 32 * NZ), 1)
    k, q = r & 3, lax.axis_index("gy")
    used = (r >> 2) * 32 + ((4 * q + k + jnp.where(k < 2, -2, 2)) & 31)
    take = jnp.where(col == used, 1.0, 0.0).astype(BF16)
    same = (iota((n, n), 0) >> 2) == (iota((n, n), 1) >> 2)
    col, ln = iota((32, n), 0), iota((32, n), 1)
    for half, ref in zip(halves(y_ref[...]), (hi_ref, lo_ref)):
        mine = jnp.dot(take, half, preferred_element_type=F32).astype(BF16)
        for p in range(8):
            pick = jnp.where(col == 4 * p + ((ln + 2) & 3), 1.0, 0.0).astype(BF16)
            full = jnp.dot(mine, pick, preferred_element_type=F32)
            ref[:, n * p:n * (p + 1)] = jnp.where(same, full, 0.0).astype(BF16)


def rims_kernel(wrim_ref, cx_ref, byr_ref, sx_ref, out_ref):
    n = 4 * NZ
    same = (iota((n, n), 0) >> 2) == (iota((n, n), 1) >> 2)
    mixed = jnp.where(same, dot3(cx_ref[...], byr_ref[...], ((1,), (1,))), 0.0)
    v = wrim_ref[...] - dot3(sx_ref[...], mixed, ((0,), (0,)))
    for q in range(8):
        out_ref[q] = v


def spread(packed, g):
    lane = iota((CX, CY), 1)
    return jnp.concatenate([jnp.where((lane >> 2) == STEP * g + i, packed, 0.0) for i in range(STEP)])


def couple_kernel(lin_hbm, by_hbm, cx_ref, sx_ref, u_hbm, lin, by, u, spikes, sems):
    for g in range(NZ // STEP):
        piece(lin_hbm, lin, sems.at[0], g).start()
        piece(by_hbm, by, sems.at[1], g).start()
    spikes[...] = jnp.transpose(sx_ref[...])

    def step(h, carry):
        for g in (2 * h, 2 * h + 1):
            fix = dot3(spread(spikes[...], g), cx_ref[...], ((1,), (0,)))
            piece(lin_hbm, lin, sems.at[0], g).wait()
            piece(by_hbm, by, sems.at[1], g).wait()
            for i in range(STEP):
                z = STEP * g + i
                vs = jnp.concatenate(halves(lin[z] - fix[CX * i:CX * (i + 1)]))
                bs = jnp.concatenate(halves(by[z]))
                all_ = lax.dot_general(vs, bs, (((1,), (1,)), ((), ())), preferred_element_type=F32)
                u[z] = all_[:CX, :CY] + (all_[:CX, CY:] + all_[CX:, :CY])
            piece(u, u_hbm, sems.at[2], g).start()
        return carry

    lax.fori_loop(0, NZ // STEP // 2, step, 0)
    for g in range(NZ // STEP):
        piece(u, u_hbm, sems.at[2], g).wait()


def last_kernel(u_hbm, g_ref, dh_ref, dl_ref, sy_ref, out_hbm, u, cy, sems):
    nt = lambda a, b: lax.dot_general(a, b, (((1,), (1,)), ((), ())), preferred_element_type=F32)
    for g in range(NZ // STEP):
        piece(u_hbm, u, sems.at[0], g).start()
    gh, gl = halves(jnp.concatenate([g_ref[q] for q in range(8)], axis=1))
    cy[...] = nt(gh, dh_ref[...]) + (nt(gh, dl_ref[...]) + nt(gl, dh_ref[...]))

    def step(g, carry):
        fix = dot3(spread(cy[...], g), sy_ref[...], ((1,), (0,)))
        piece(u_hbm, u, sems.at[0], g).wait()
        for i in range(STEP):
            z = STEP * g + i
            u[z] = u[z] - fix[CX * i:CX * (i + 1)]
        piece(u, out_hbm, sems.at[1], g).start()
        return carry

    lax.fori_loop(0, NZ // STEP, step, 0)
    for g in range(NZ // STEP):
        piece(u, out_hbm, sems.at[1], g).wait()


def shape(*dims):
    return jax.ShapeDtypeStruct(dims, F32)


def body(conc, mobility, block_x, spike_x, reduced_x, block_y, spike_y, reduced_y):
    nx, ny = lax.axis_size("gx"), lax.axis_size("gy")
    p = lax.axis_index("gx")
    hbm = lambda a: pltpu.with_memory_space_constraint(a, pltpu.HBM)
    any_space = pl.BlockSpec(memory_space=pl.ANY)
    here = pl.BlockSpec()
    full = lambda *dims: pltpu.VMEM(dims, F32)
    groups = NZ // STEP
    big, big_hbm = shape(NZ, CX, CY), pltpu.HBM((NZ, CX, CY), F32)

    def pairs(n, start):
        ends = [(i % n, (i + 1) % n) for i in range(start, start + n, 2)]
        return ends + [(b, a) for a, b in ends]

    def swap(first, second, axis, n):
        return lax.ppermute(first, axis, pairs(n, 0)), lax.ppermute(second, axis, pairs(n, 1))

    own0, own1 = pl.pallas_call(
        edge_kernel,
        in_specs=[any_space, any_space],
        out_shape=(shape(3 * NZ, CY), shape(3 * NZ, CY)),
        scratch_shapes=[full(NZ, 8, CY)] * 4 + [pltpu.SemaphoreType.DMA((4,))],
        compiler_params=CALL, name="edge",
    )(hbm(conc), hbm(mobility))
    got0, got1 = swap(own0, own1, "gx", nx)
    *side, mu, mobx, moby = pl.pallas_call(
        pack_kernel,
        out_shape=(shape(CX, CY),) * 2 + (shape(NZ, CX, CY),) * 3,
        compiler_params=CALL, name="pack",
    )(conc, mobility)
    send0, send1 = pl.pallas_call(
        corner_kernel, out_shape=(shape(72, CY),) * 2, compiler_params=CALL, name="corner"
    )(*side, got0, got1)
    side0, side1 = swap(send0, send1, "gy", ny)

    lin, rims = pl.pallas_call(
        lines_kernel,
                out_specs=(any_space, any_space),
        out_shape=(big_hbm, pltpu.HBM((NZ, 4, CY), F32)),
        scratch_shapes=[full(NZ, CX, CY), full(NZ, 4, CY)]
        + [full(CX, CY)] * 2 + [full(NZ, CY)] * 4 + [full(72, CY)] * 4 + [full(3 * NZ, CY)] * 2
        + [pltpu.SemaphoreType.DMA((2, 2 * groups))],
        compiler_params=CALL, name="lines",
    )(conc, mu, mobx, moby, block_x, own0, own1, send0, send1, side0, side1, got0, got1)

    lin, rims, block_y, reduced_y = lax.optimization_barrier((lin, rims, block_y, reduced_y))
    sx = jnp.transpose(spike_x, (0, 2, 1)).reshape(4 * NZ, CX)
    sy = jnp.transpose(spike_y, (0, 2, 1)).reshape(4 * NZ, CY)
    wrim, byr = pl.pallas_call(
        wide_kernel,
        in_specs=[any_space] * 2,
        out_shape=(shape(CX, CY), shape(4 * NZ, CY)),
        scratch_shapes=[full(NZ, CX, CY)] + [full(NZ, 8, CY)] * 2 + [pltpu.SemaphoreType.DMA((groups + 2,))],
        compiler_params=CALL, name="wide",
    )(hbm(lin), hbm(block_y))
    dh, dl = pl.pallas_call(
        diag_kernel,
        out_shape=(jax.ShapeDtypeStruct((CY, ny * CY), BF16),) * 2,
        compiler_params=CALL, name="diag",
    )(reduced_y.reshape(NZ * 4 * ny, 4 * ny))

    mine = lax.dynamic_index_in_dim(reduced_x, p, 0, keepdims=False)
    rims = lax.all_to_all(rims, "gx", 0, 0, tiled=True)
    rims, wrim, mine = lax.optimization_barrier((rims, wrim, mine))
    solved = pl.pallas_call(
        reduced_kernel, out_shape=shape(4 * NZ, CY), compiler_params=CALL, name="reduced"
    )(mine, rims.reshape(4 * NZ, CY))
    cx = lax.all_to_all(solved.reshape(NZ, 4, CY), "gx", 0, 0, tiled=True).reshape(4 * NZ, CY)

    yrim = pl.pallas_call(rims_kernel, out_shape=shape(ny, CX, CY), compiler_params=CALL, name="rims")(
        wrim, cx, byr, sx
    )
    yall = lax.all_to_all(yrim, "gy", 0, 0, tiled=True)
    u = pl.pallas_call(
        couple_kernel,
        in_specs=[any_space, any_space, here, here],
        out_specs=any_space,
        out_shape=big_hbm,
        scratch_shapes=[full(NZ, CX, CY), full(NZ, CY, CY), full(NZ, CX, CY), full(CX, CY),
                        pltpu.SemaphoreType.DMA((3, groups))],
        compiler_params=CALL, name="couple",
    )(hbm(lin), hbm(block_y), cx, sx)
    return pl.pallas_call(
        last_kernel,
        in_specs=[any_space] + [here] * 4,
        out_specs=any_space,
        out_shape=big_hbm,
        scratch_shapes=[full(NZ, CX, CY), full(CX, CY), pltpu.SemaphoreType.DMA((2, groups))],
        compiler_params=CALL, name="last",
    )(hbm(u), yall, dh, dl, sy)


def solution(mesh):
    in_specs = (
        P(None, "gx", "gy"),
        P(None, "gx", "gy"),
        P(None, "gx", None),
        P(None, "gx", None),
        P(),
        P(None, "gy", None),
        P(None, "gy", None),
        P(),
    )
    out_specs = P(None, "gx", "gy")
    return jax.shard_map(body, mesh=mesh, in_specs=in_specs, out_specs=out_specs, check_vma=False)
```

```python
import jax
import jax.numpy as jnp
from jax import lax
from jax.experimental import pallas as pl
from jax.experimental.pallas import tpu as pltpu
from jax.sharding import PartitionSpec as P

NZ, CX, CY = 32, 64, 128
STEP, HALF = 8, 2
F32, BF16 = jnp.float32, jnp.bfloat16
CALL = pltpu.CompilerParams(vmem_limit_bytes=12 * 1024 * 1024)


def halves(a):
    hi = a.astype(BF16)
    return hi, (a - hi.astype(F32)).astype(BF16)


def dot3(a, b, dims):
    ah, al = halves(a)
    bh, bl = halves(b)
    one = lambda x, y: lax.dot_general(x, y, (dims, ((), ())), preferred_element_type=F32)
    return one(ah, bh) + (one(ah, bl) + one(al, bh))


def iota(shape, axis):
    return lax.broadcasted_iota(jnp.int32, shape, axis)


def roll(a, shift, axis):
    if isinstance(shift, int) and shift % a.shape[axis] == 0:
        return a
    if isinstance(shift, int):
        shift = shift % a.shape[axis]
    return pltpu.roll(a, shift, axis)


def potential(c, lap):
    return c * c * c - c - lap


def mobile(prefactor, c):
    sq = c * c
    return prefactor * (0.25 + sq) / (1.0 + sq)


def odd_at(axis):
    return (lax.axis_index(axis) & 1) == 1


def edge_kernel(c_ref, m_ref, first_ref, second_ref, ct, cb, mt, mb, sems):
    top, bottom = pl.ds(0, 8), pl.ds(CX - 8, 8)
    copies = [
        pltpu.make_async_copy(c_ref.at[:, top, :], ct, sems.at[0]),
        pltpu.make_async_copy(m_ref.at[:, top, :], mt, sems.at[1]),
        pltpu.make_async_copy(c_ref.at[:, bottom, :], cb, sems.at[2]),
        pltpu.make_async_copy(m_ref.at[:, bottom, :], mb, sems.at[3]),
    ]
    for copy in copies:
        copy.start()
    for copy in copies:
        copy.wait()
    odd = odd_at("gx")
    rows = ((ct[:, 0, :], cb[:, 7, :]), (ct[:, 1, :], cb[:, 6, :]), (mt[:, 0, :], mb[:, 7, :]))
    for k, (lo, hi) in enumerate(rows):
        first_ref[NZ * k:NZ * (k + 1)] = jnp.where(odd, lo, hi)
        second_ref[NZ * k:NZ * (k + 1)] = jnp.where(odd, hi, lo)


def pack_kernel(c_ref, m_ref, first_ref, second_ref, mu_ref, mobx_ref, moby_ref):
    row, lane = iota((CX, CY), 0), iota((CX, CY), 1)
    lo = jnp.zeros((CX, CY), F32)
    hi = jnp.zeros((CX, CY), F32)
    for z in range(NZ):
        c = roll(c_ref[z], 4 * z, 1)
        m = roll(m_ref[z], 4 * z + 2, 1)
        a, b = (4 * z - 2) % CY, 4 * z
        lo = jnp.where((lane >= b) & (lane <= b + 1), c, lo)
        lo = jnp.where(lane == b + 2, m, lo)
        hi = jnp.where((lane >= a) & (lane <= a + 1), c, hi)
        hi = jnp.where(lane == b + 1, m, hi)
    odd = odd_at("gy")
    first_ref[...] = jnp.where(odd, lo, hi)
    second_ref[...] = jnp.where(odd, hi, lo)

    def step(g, carry):
        for i in range(STEP):
            z = g * STEP + i
            c = c_ref[z]
            up = jnp.where(row == 0, 0.0, roll(c, 1, 0))
            down = jnp.where(row == CX - 1, 0.0, roll(c, -1, 0))
            lf = jnp.where(lane == 0, 0.0, roll(c, 1, 1))
            rt = jnp.where(lane == CY - 1, 0.0, roll(c, -1, 1))
            mu_ref[z] = potential(c, up + down + lf + rt - 4.0 * c)
            mob = mobile(m_ref[z], c)
            mobx_ref[z] = mob + roll(mob, -1, 0)
            moby_ref[z] = mob + roll(mob, -1, 1)
        return carry

    lax.fori_loop(0, NZ // STEP, step, 0)


def corner_kernel(side0_ref, side1_ref, got0_ref, got1_ref, first_ref, second_ref):
    sub, lane = iota((NZ, CY), 0), iota((NZ, CY), 1)
    odd_x, odd_y = odd_at("gx"), odd_at("gy")
    got0, got1 = got0_ref[0:NZ], got1_ref[0:NZ]
    up, down = jnp.where(odd_x, got0, got1), jnp.where(odd_x, got1, got0)
    pad = jnp.zeros((6, CY), F32)

    def rows(k, at):
        pick = lambda a: jnp.sum(jnp.where(lane == at, a[:, k:k + 1], 0.0), axis=0, keepdims=True)
        return jnp.concatenate([pick(up), pick(down), pad])

    lo, hi = rows(0, 4 * sub), rows(CY - 1, (4 * sub - 1) & (CY - 1))
    first_ref[0:CX] = side0_ref[...]
    second_ref[0:CX] = side1_ref[...]
    first_ref[CX:72] = jnp.where(odd_y, lo, hi)
    second_ref[CX:72] = jnp.where(odd_y, hi, lo)


def piece(src, dst, sems, g, size=STEP):
    at = pl.ds(g * size, size)
    return pltpu.make_async_copy(src.at[at], dst.at[at], sems.at[g])


def lines_kernel(c_ref, mu_ref, mobx_ref, moby_ref, bx_ref, own0_ref, own1_ref, send0_ref, send1_ref, side0_ref, side1_ref, got0_ref,
                 got1_ref, lin_hbm, rim_hbm, lin_ref, rim_ref, ch, fh, mul, mobl, mur, mobr, slo_ref,
                 shi_ref, yl_ref, yr_ref, xl_ref, xr_ref, sems):
    row, row8 = iota((CX, CY), 0), iota((8, CY), 0)
    lane = iota((CX, CY), 1)
    odd_x, odd_y = odd_at("gx"), odd_at("gy")

    def edges():
        slo_ref[...] = jnp.where(odd_y, send0_ref[...], send1_ref[...])
        shi_ref[...] = jnp.where(odd_y, send1_ref[...], send0_ref[...])
        yl_ref[...] = jnp.where(odd_y, side0_ref[...], side1_ref[...])
        yr_ref[...] = jnp.where(odd_y, side1_ref[...], side0_ref[...])
        xl_ref[...] = jnp.where(odd_x, got0_ref[...], got1_ref[...])
        xr_ref[...] = jnp.where(odd_x, got1_ref[...], got0_ref[...])
        own_lo = jnp.where(odd_x, own0_ref[...], own1_ref[...])
        own_hi = jnp.where(odd_x, own1_ref[...], own0_ref[...])
        lo, hi, left, right = slo_ref[0:CX], shi_ref[0:CX], yl_ref[0:CX], yr_ref[0:CX]

        def around(a, ref):
            up = jnp.where(row == 0, ref[CX:CX + 1], roll(a, 1, 0))
            down = jnp.where(row == CX - 1, ref[CX + 1:CX + 2], roll(a, -1, 0))
            return up + down

        c0, c1, m0 = lo, roll(lo, -1, 1), roll(lo, -2, 1)
        cm1, cm2, mm1 = roll(left, 1, 1), roll(left, 2, 1), roll(left, -1, 1)
        mu0 = potential(c0, cm1 + c1 + around(lo, slo_ref) - 4.0 * c0)
        mum1 = potential(cm1, cm2 + c0 + roll(around(left, yl_ref), 1, 1) - 4.0 * cm1)
        flux_l = (mobile(mm1, cm1) + mobile(m0, c0)) * (mu0 - mum1)
        cn, cn1, mn = hi, roll(hi, 1, 1), roll(hi, -2, 1)
        cp, cp2, mp = roll(right, -1, 1), roll(right, -2, 1), roll(right, -3, 1)
        mun = potential(cn, cn1 + cp + around(hi, shi_ref) - 4.0 * cn)
        mup = potential(cp, cn + cp2 + roll(around(right, yr_ref), -1, 1) - 4.0 * cp)
        flux_r = (mobile(mp, cp) + mobile(mn, cn)) * (mup - mun)
        first = (lane & 3) == 0
        fh[...] = jnp.where(first, flux_l, flux_r)
        ch[...] = jnp.where(first, cm1, cp)

        sub, ln = iota((NZ, CY), 0), iota((NZ, CY), 1)

        def halo_row(x_ref, own, k, mu_out, mob_out):
            a = x_ref[0:32]
            west = jnp.where(ln == ((4 * sub - 1) & (CY - 1)), yl_ref[CX + k:CX + k + 1], 0.0)
            east = jnp.where(ln == 4 * sub, yr_ref[CX + k:CX + k + 1], 0.0)
            lf = jnp.where(ln == 0, jnp.sum(west, axis=1, keepdims=True), roll(a, 1, 1))
            rt = jnp.where(ln == CY - 1, jnp.sum(east, axis=1, keepdims=True), roll(a, -1, 1))
            mu_out[...] = potential(a, x_ref[32:64] + own[0:32] + lf + rt - 4.0 * a)
            mob_out[...] = mobile(x_ref[64:96], a) + mobile(own[64:96], own[0:32])

        halo_row(xl_ref, own_lo, 0, mul, mobl)
        halo_row(xr_ref, own_hi, 1, mur, mobr)

    edges()

    def step(g, carry):
        for i in range(STEP):
            plane(g * STEP + i)
            if i % HALF == HALF - 1:
                piece(lin_ref, lin_hbm, sems.at[0], (STEP // HALF) * g + i // HALF, HALF).start()
                piece(rim_ref, rim_hbm, sems.at[1], (STEP // HALF) * g + i // HALF, HALF).start()
        return carry

    def plane(z):
        at = pl.ds(z, 1)
        turn = (CY - 4 * z) & (CY - 1)
        c, mobx = c_ref[z], mobx_ref[z]
        hz = roll(ch[...], turn, 1)
        fz = roll(fh[...], turn, 1)
        mu = mu_ref[z] - jnp.where((lane == 0) | (lane == CY - 1), hz, 0.0)
        mu = jnp.concatenate([
            mu[0:8] - jnp.where(row8 == 0, xl_ref[at], 0.0),
            mu[8:CX - 8],
            mu[CX - 8:CX] - jnp.where(row8 == 7, xr_ref[at], 0.0),
        ])
        mu_d = jnp.where(row == CX - 1, mur[at], roll(mu, -1, 0))
        mobx = jnp.concatenate([mobx[:CX - 8], jnp.where(row8 == 7, mobr[at], mobx[CX - 8:])])
        fx = mobx * (mu_d - mu)
        f0 = mobl[at] * (mu[0:1] - mul[at])
        fx_up = jnp.where(row == 0, f0, roll(fx, 1, 0))
        fy = moby_ref[z] * (roll(mu, -1, 1) - mu)
        fy = jnp.where(lane == CY - 1, fz, fy)
        fy_lf = jnp.where(lane == 0, fz, roll(fy, 1, 1))
        rhs = c + 0.01 * ((fx - fx_up) + (fy - fy_lf))
        lin = dot3(bx_ref[z], rhs, ((1,), (0,)))
        lin_ref[z] = lin
        rim_ref[z, 0:2] = lin[0:2]
        rim_ref[z, 2:4] = lin[CX - 2:CX]

    lax.fori_loop(0, NZ // STEP, step, 0)
    for g in range(NZ // HALF):
        piece(lin_ref, lin_hbm, sems.at[0], g, HALF).wait()
        piece(rim_ref, rim_hbm, sems.at[1], g, HALF).wait()


def reduced_kernel(r_ref, rim_ref, out_ref):
    r = r_ref[...]
    use = jnp.where((iota((4 * NZ, 4 * NZ), 0) & 3) < 2, roll(r, 2, 0), roll(r, -2, 0))
    out_ref[...] = dot3(use, rim_ref[...], ((1,), (0,)))


def wide_kernel(lin_hbm, by_hbm, rim_ref, byr_ref, lin, low, high, sems):
    ends = [
        pltpu.make_async_copy(by_hbm.at[:, pl.ds(0, 8), :], low, sems.at[NZ // STEP]),
        pltpu.make_async_copy(by_hbm.at[:, pl.ds(CY - 8, 8), :], high, sems.at[NZ // STEP + 1]),
    ]
    for copy in ends:
        copy.start()
    for g in range(NZ // STEP):
        piece(lin_hbm, lin, sems, g).start()
    for copy in ends:
        copy.wait()
    for k in range(4):
        byr_ref[pl.ds(k, NZ, stride=4), :] = high[:, 6 + k, :] if k < 2 else low[:, k - 2, :]
    lane = iota((CX, CY), 1)
    acc = jnp.zeros((CX, CY), F32)
    for g in range(NZ // STEP):
        piece(lin_hbm, lin, sems, g).wait()
        part = lin[STEP * g:STEP * (g + 1)].reshape(STEP * CX, CY)
        out = dot3(part, byr_ref[...], ((1,), (1,)))
        for i in range(STEP):
            acc = jnp.where((lane >> 2) == STEP * g + i, out[CX * i:CX * (i + 1)], acc)
    rim_ref[...] = acc


def diag_kernel(y_ref, hi_ref, lo_ref):
    n = 4 * NZ
    r, col = iota((n, 32 * NZ), 0), iota((n, 32 * NZ), 1)
    k, q = r & 3, lax.axis_index("gy")
    used = (r >> 2) * 32 + ((4 * q + k + jnp.where(k < 2, -2, 2)) & 31)
    take = jnp.where(col == used, 1.0, 0.0).astype(BF16)
    same = (iota((n, n), 0) >> 2) == (iota((n, n), 1) >> 2)
    col, ln = iota((32, n), 0), iota((32, n), 1)
    for half, ref in zip(halves(y_ref[...]), (hi_ref, lo_ref)):
        mine = jnp.dot(take, half, preferred_element_type=F32).astype(BF16)
        for p in range(8):
            pick = jnp.where(col == 4 * p + ((ln + 2) & 3), 1.0, 0.0).astype(BF16)
            full = jnp.dot(mine, pick, preferred_element_type=F32)
            ref[:, n * p:n * (p + 1)] = jnp.where(same, full, 0.0).astype(BF16)


def rims_kernel(wrim_ref, cx_ref, byr_ref, sx_ref, out_ref):
    n = 4 * NZ
    same = (iota((n, n), 0) >> 2) == (iota((n, n), 1) >> 2)
    mixed = jnp.where(same, dot3(cx_ref[...], byr_ref[...], ((1,), (1,))), 0.0)
    v = wrim_ref[...] - dot3(sx_ref[...], mixed, ((0,), (0,)))
    for q in range(8):
        out_ref[q] = v


def spread(packed, g):
    lane = iota((CX, CY), 1)
    return jnp.concatenate([jnp.where((lane >> 2) == STEP * g + i, packed, 0.0) for i in range(STEP)])


def couple_kernel(lin_hbm, by_hbm, cx_ref, sx_ref, u_hbm, lin, by, u, spikes, sems):
    for g in range(NZ // STEP):
        piece(lin_hbm, lin, sems.at[0], g).start()
        piece(by_hbm, by, sems.at[1], g).start()
    spikes[...] = jnp.transpose(sx_ref[...])

    def step(h, carry):
        for g in (2 * h, 2 * h + 1):
            fix = dot3(spread(spikes[...], g), cx_ref[...], ((1,), (0,)))
            piece(lin_hbm, lin, sems.at[0], g).wait()
            piece(by_hbm, by, sems.at[1], g).wait()
            for i in range(STEP):
                z = STEP * g + i
                vs = jnp.concatenate(halves(lin[z] - fix[CX * i:CX * (i + 1)]))
                bs = jnp.concatenate(halves(by[z]))
                all_ = lax.dot_general(vs, bs, (((1,), (1,)), ((), ())), preferred_element_type=F32)
                u[z] = all_[:CX, :CY] + (all_[:CX, CY:] + all_[CX:, :CY])
            piece(u, u_hbm, sems.at[2], g).start()
        return carry

    lax.fori_loop(0, NZ // STEP // 2, step, 0)
    for g in range(NZ // STEP):
        piece(u, u_hbm, sems.at[2], g).wait()


def last_kernel(u_hbm, g_ref, dh_ref, dl_ref, sy_ref, out_hbm, u, cy, sems):
    nt = lambda a, b: lax.dot_general(a, b, (((1,), (1,)), ((), ())), preferred_element_type=F32)
    for g in range(NZ // STEP):
        piece(u_hbm, u, sems.at[0], g).start()
    gh, gl = halves(jnp.concatenate([g_ref[q] for q in range(8)], axis=1))
    cy[...] = nt(gh, dh_ref[...]) + (nt(gh, dl_ref[...]) + nt(gl, dh_ref[...]))

    def step(g, carry):
        fix = dot3(spread(cy[...], g), sy_ref[...], ((1,), (0,)))
        piece(u_hbm, u, sems.at[0], g).wait()
        for i in range(STEP):
            z = STEP * g + i
            u[z] = u[z] - fix[CX * i:CX * (i + 1)]
        piece(u, out_hbm, sems.at[1], g).start()
        return carry

    lax.fori_loop(0, NZ // STEP, step, 0)
    for g in range(NZ // STEP):
        piece(u, out_hbm, sems.at[1], g).wait()


def shape(*dims):
    return jax.ShapeDtypeStruct(dims, F32)


def body(conc, mobility, block_x, spike_x, reduced_x, block_y, spike_y, reduced_y):
    nx, ny = lax.axis_size("gx"), lax.axis_size("gy")
    p = lax.axis_index("gx")
    hbm = lambda a: pltpu.with_memory_space_constraint(a, pltpu.HBM)
    any_space = pl.BlockSpec(memory_space=pl.ANY)
    here = pl.BlockSpec()
    full = lambda *dims: pltpu.VMEM(dims, F32)
    groups = NZ // STEP
    big, big_hbm = shape(NZ, CX, CY), pltpu.HBM((NZ, CX, CY), F32)

    def pairs(n, start):
        ends = [(i % n, (i + 1) % n) for i in range(start, start + n, 2)]
        return ends + [(b, a) for a, b in ends]

    def swap(first, second, axis, n):
        return lax.ppermute(first, axis, pairs(n, 0)), lax.ppermute(second, axis, pairs(n, 1))

    own0, own1 = pl.pallas_call(
        edge_kernel,
        in_specs=[any_space, any_space],
        out_shape=(shape(3 * NZ, CY), shape(3 * NZ, CY)),
        scratch_shapes=[full(NZ, 8, CY)] * 4 + [pltpu.SemaphoreType.DMA((4,))],
        compiler_params=CALL, name="edge",
    )(hbm(conc), hbm(mobility))
    got0, got1 = swap(own0, own1, "gx", nx)
    *side, mu, mobx, moby = pl.pallas_call(
        pack_kernel,
        out_shape=(shape(CX, CY),) * 2 + (shape(NZ, CX, CY),) * 3,
        compiler_params=CALL, name="pack",
    )(conc, mobility)
    send0, send1 = pl.pallas_call(
        corner_kernel, out_shape=(shape(72, CY),) * 2, compiler_params=CALL, name="corner"
    )(*side, got0, got1)
    side0, side1 = swap(send0, send1, "gy", ny)

    lin, rims = pl.pallas_call(
        lines_kernel,
                out_specs=(any_space, any_space),
        out_shape=(big_hbm, pltpu.HBM((NZ, 4, CY), F32)),
        scratch_shapes=[full(NZ, CX, CY), full(NZ, 4, CY)]
        + [full(CX, CY)] * 2 + [full(NZ, CY)] * 4 + [full(72, CY)] * 4 + [full(3 * NZ, CY)] * 2
        + [pltpu.SemaphoreType.DMA((2, NZ // HALF))],
        compiler_params=CALL, name="lines",
    )(conc, mu, mobx, moby, block_x, own0, own1, send0, send1, side0, side1, got0, got1)

    lin, rims, block_y, reduced_y = lax.optimization_barrier((lin, rims, block_y, reduced_y))
    sx = jnp.transpose(spike_x, (0, 2, 1)).reshape(4 * NZ, CX)
    sy = jnp.transpose(spike_y, (0, 2, 1)).reshape(4 * NZ, CY)
    wrim, byr = pl.pallas_call(
        wide_kernel,
        in_specs=[any_space] * 2,
        out_shape=(shape(CX, CY), shape(4 * NZ, CY)),
        scratch_shapes=[full(NZ, CX, CY)] + [full(NZ, 8, CY)] * 2 + [pltpu.SemaphoreType.DMA((groups + 2,))],
        compiler_params=CALL, name="wide",
    )(hbm(lin), hbm(block_y))
    dh, dl = pl.pallas_call(
        diag_kernel,
        out_shape=(jax.ShapeDtypeStruct((CY, ny * CY), BF16),) * 2,
        compiler_params=CALL, name="diag",
    )(reduced_y.reshape(NZ * 4 * ny, 4 * ny))

    mine = lax.dynamic_index_in_dim(reduced_x, p, 0, keepdims=False)
    rims = lax.all_to_all(rims, "gx", 0, 0, tiled=True)
    rims, wrim, mine = lax.optimization_barrier((rims, wrim, mine))
    solved = pl.pallas_call(
        reduced_kernel, out_shape=shape(4 * NZ, CY), compiler_params=CALL, name="reduced"
    )(mine, rims.reshape(4 * NZ, CY))
    cx = lax.all_to_all(solved.reshape(NZ, 4, CY), "gx", 0, 0, tiled=True).reshape(4 * NZ, CY)

    yrim = pl.pallas_call(rims_kernel, out_shape=shape(ny, CX, CY), compiler_params=CALL, name="rims")(
        wrim, cx, byr, sx
    )
    yall = lax.all_to_all(yrim, "gy", 0, 0, tiled=True)
    u = pl.pallas_call(
        couple_kernel,
        in_specs=[any_space, any_space, here, here],
        out_specs=any_space,
        out_shape=big_hbm,
        scratch_shapes=[full(NZ, CX, CY), full(NZ, CY, CY), full(NZ, CX, CY), full(CX, CY),
                        pltpu.SemaphoreType.DMA((3, groups))],
        compiler_params=CALL, name="couple",
    )(hbm(lin), hbm(block_y), cx, sx)
    return pl.pallas_call(
        last_kernel,
        in_specs=[any_space] + [here] * 4,
        out_specs=any_space,
        out_shape=big_hbm,
        scratch_shapes=[full(NZ, CX, CY), full(CX, CY), pltpu.SemaphoreType.DMA((2, groups))],
        compiler_params=CALL, name="last",
    )(hbm(u), yall, dh, dl, sy)


def solution(mesh):
    in_specs = (
        P(None, "gx", "gy"),
        P(None, "gx", "gy"),
        P(None, "gx", None),
        P(None, "gx", None),
        P(),
        P(None, "gy", None),
        P(None, "gy", None),
        P(),
    )
    out_specs = P(None, "gx", "gy")
    return jax.shard_map(body, mesh=mesh, in_specs=in_specs, out_specs=out_specs, check_vma=False)
```
